128 devices in a mesh: leaf: 8 (over z, core), rows: 16 (over y, x).
Axes of the slice: x: 4, y: 4, z: 4, core: 2. Of those that a mesh axis runs over, the one named last changes fastest.
Arguments:
- rhs: bfloat16 [589824, 512], P(('leaf', 'rows')), may hold values from -6 to 6
- leaf_order: int32 [2304, 256], P(('leaf', 'rows')), may hold values from 0 to 255, each once within a row
- leaf_inv: bfloat16 [2304, 256, 256], P(('leaf', 'rows')), may hold values from -0.375 to 0.375
- right_basis: bfloat16 [4, 589824, 128], P(None, ('leaf', 'rows')), may hold values from -0.0234375 to 0.0234375
- left_basis: bfloat16 [4, 589824, 128], P(None, ('leaf', 'rows')), may hold values from -0.375 to 0.375
- rank_perm: int32 [4, 128], replicated, may hold values from 0 to 127, each once within a row
- joined: float32 [15, 256, 256], replicated, may hold values from -0.375 to 0.375
Outputs:
- solution: float32 [589824, 512], P(('leaf', 'rows'))
The draws below stay inside these ranges and needn't reach their ends.
Inputs may be any that keep to these rules, and one draw needn't show every extreme that they name: Each row of leaf_order names every number below 256 once. Each row of rank_perm names every number below 128 once.
All inputs are finite; a program needn't handle non-finite values.
Results may differ from the reference program's by a relative error of at most 0.0003.
Values sent between devices are 32-bit elements; how exact they have to be, the bound alone decides.
A program may use at most 128 MiB of HBM per device.

```python
import jax
import jax.numpy as jnp
from jax import lax

BLOCK_ORDER = 256
RANK_WIDTH = 128
TARGETS = 512
ROWS_DEV = 4608
LEVELS = 4
ROW_BITS = 4
NODE_COUNT = 15
TOTAL_ROWS = 589824
BLOCK_COUNT = 2304
N_ROWS = 16


def shard_levels(stream_key, dims, pieces, smallest, high):
    def one(position, shards_of):
        draws = jax.random.uniform(jax.random.fold_in(jax.random.fold_in(stream_key, 6), position), (shards_of,), jnp.float32, smallest / len(pieces), high / len(pieces))
        return jnp.repeat(jnp.exp(draws), dims[position] // shards_of).reshape((-1,) + (1,) * (len(dims) - position - 1))

    level = one(*pieces[0])
    for cut in pieces[1:]:
        level = level * one(*cut)
    return level


def gaussian(stream_key, extent, spread, most, split=(), kind=jnp.bfloat16):
    entries = jax.random.normal(stream_key, extent, jnp.float32) * spread
    if len(split) > 0:
        entries = shard_levels(stream_key, extent, split, -0.22, 0.18) * entries
    return jnp.clip(entries, min=-most, max=most).astype(kind)


def setup_inputs(seed: int = 0) -> dict:
    splits = jax.random.split(jax.random.key(seed), 8)
    rhs = gaussian(splits[0], (TOTAL_ROWS, TARGETS), 1.0, 6.0, ((0, 128),))
    leaf_order = jax.vmap(lambda own: jax.random.permutation(own, BLOCK_ORDER))(jax.random.split(splits[1], BLOCK_COUNT)).reshape((BLOCK_COUNT, BLOCK_ORDER)).astype(jnp.int32)
    leaf_inv = gaussian(splits[2], (BLOCK_COUNT, BLOCK_ORDER, BLOCK_ORDER), BLOCK_ORDER ** -0.5, 0.375, ((0, 128),))
    right_basis = gaussian(splits[3], (LEVELS, TOTAL_ROWS, RANK_WIDTH), (ROWS_DEV * N_ROWS) ** -0.5, 0.0234375, ((1, 128),))
    left_basis = gaussian(splits[4], (LEVELS, TOTAL_ROWS, RANK_WIDTH), (2 * RANK_WIDTH) ** -0.5, 0.375, ((1, 128),))
    rank_perm = jax.vmap(lambda own: jax.random.permutation(own, RANK_WIDTH))(jax.random.split(splits[5], LEVELS)).reshape((LEVELS, RANK_WIDTH)).astype(jnp.int32)
    joined = gaussian(splits[6], (NODE_COUNT, 2 * RANK_WIDTH, 2 * RANK_WIDTH), (2 * RANK_WIDTH) ** -0.5, 0.375, (), jnp.float32)
    return dict(rhs=rhs, leaf_order=leaf_order, leaf_inv=leaf_inv, right_basis=right_basis, left_basis=left_basis, rank_perm=rank_perm, joined=joined)


HIGHEST = lax.Precision.HIGHEST


def reference(rhs, leaf_order, leaf_inv, right_basis, left_basis, rank_perm, joined):
    block_count = leaf_inv.shape[0]
    blocks = rhs.reshape(block_count, BLOCK_ORDER, TARGETS)
    ordered = jnp.take_along_axis(blocks, leaf_order[:, :, None], axis=1)
    current = jnp.einsum("bij,bjr->bir", leaf_inv.astype(jnp.float32), ordered.astype(jnp.float32),
                         precision=HIGHEST).reshape(TOTAL_ROWS, TARGETS)
    for tree_level in range(LEVELS):
        child_rows = ROWS_DEV * 2 ** (ROW_BITS - 1 + tree_level)
        children = TOTAL_ROWS // child_rows
        right_rows = right_basis[tree_level].astype(jnp.float32).reshape(children, child_rows, RANK_WIDTH)
        projection = jnp.einsum("cmk,cmr->ckr", right_rows, current.reshape(children, child_rows, TARGETS),
                                precision=HIGHEST)
        picked = projection[:, rank_perm[tree_level], :]
        offset = NODE_COUNT + 1 - (NODE_COUNT + 1) // 2 ** tree_level
        node_inverse = joined[offset:offset + children // 2]
        stacked = picked.reshape(children // 2, 2 * RANK_WIDTH, TARGETS)
        coefficient = jnp.einsum("nij,njr->nir", node_inverse, stacked,
                                 precision=HIGHEST).reshape(children, RANK_WIDTH, TARGETS)
        left_rows = left_basis[tree_level].astype(jnp.float32).reshape(children, child_rows, RANK_WIDTH)
        update = jnp.einsum("cmk,ckr->cmr", left_rows, coefficient, precision=HIGHEST)
        current = current - update.reshape(TOTAL_ROWS, TARGETS)
    return current
```

```python
import functools

import jax
import jax.numpy as jnp
from jax import lax
from jax.experimental import pallas as pl
from jax.experimental.pallas import tpu as pltpu
from jax.sharding import PartitionSpec as P

F32 = jnp.float32
BF16 = jnp.bfloat16
MESH = pl.DeviceIdType.MESH
TN = (((0,), (0,)), ((), ()))
NT = (((1,), (1,)), ((), ()))
NN = (((1,), (0,)), ((), ()))
GRAMS = ((0, 1), (0, 2), (0, 3), (1, 2), (1, 3), (2, 3))
VMEM_LIMIT = 60 * 1024 * 1024


def mm(a, b, dims=NN):
    return lax.dot_general(a, b, dims, preferred_element_type=F32)


def halves(x):
    hi = x.astype(BF16)
    return hi, (x - hi.astype(F32)).astype(BF16)


def mm3(x, w_hi, w_lo):
    hi, lo = halves(x)
    return mm(hi, w_hi) + mm(lo, w_hi) + mm(hi, w_lo)


def one_hot(row, count):
    width = row.shape[1]
    spot = lax.broadcasted_iota(jnp.int32, (count, width), 0)
    return jnp.where(spot == jnp.broadcast_to(row, (count, width)), 1.0, 0.0).astype(BF16)


def front_kernel(
    node_ref, rhs_ref, order_ref, inv_ref, right_ref, left_ref, perm_ref, j0_ref, j1_ref, j2_ref, j3_ref,
    p_ref, gram_ref, whi_ref, wlo_ref,
):
    step = pl.program_id(0)

    @pl.when(step == 0)
    def _():
        p_ref[...] = jnp.zeros_like(p_ref)
        gram_ref[...] = jnp.zeros_like(gram_ref)
        start = 0
        for level, ref in enumerate((j0_ref, j1_ref, j2_ref, j3_ref)):
            hot = one_hot(perm_ref[level : level + 1, :], 128)
            hi, lo = halves(ref[...])
            rows = hi.shape[0]
            for side in range(2):
                cut = slice(side * 128, side * 128 + 128)
                whi_ref[cut, start : start + rows] = mm(hot, hi[:, cut], NT).astype(BF16)
                wlo_ref[cut, start : start + rows] = mm(hot, lo[:, cut], NT).astype(BF16)
            start += rows

    place = one_hot(order_ref[...], 256)
    moved = mm(place, inv_ref[...], NT).astype(BF16)
    current = mm(rhs_ref[...], moved, TN)
    hi, lo = halves(current)
    for level in range(4):
        basis = right_ref[level]
        p_ref[level] += mm(hi, basis) + mm(lo, basis)
    for spot, (low, high) in enumerate(GRAMS):
        gram_ref[spot] += mm(left_ref[low], right_ref[high], TN)


def rdma(src, dst, ssem, rsem, where):
    return pltpu.make_async_remote_copy(
        src_ref=src, dst_ref=dst, send_sem=ssem, recv_sem=rsem, device_id=where, device_id_type=MESH
    )


def exchange_kernel(
    p_ref, gram_ref, whi_ref, wlo_ref, chi_ref, clo_ref,
    coef, share0, shares, rest, mine0, gparts, gsum, pair1, quad2, oct3,
    s0, r0, sg, rg, sga, rga, ss, rs, sc, rc, se1, re1, se2, re2, se3, re3,
):
    leaf = lax.axis_index("leaf")
    row = lax.axis_index("rows")

    def each_row(body):
        def step(off, carry):
            body(lax.rem(row + off, 16))
            return carry

        lax.fori_loop(1, 16, step, 0)

    def leaf_peers(count):
        base = leaf // count * count
        spot = leaf - base
        return base, spot, [lax.rem(spot + off, count) for off in range(1, count)]

    barrier = pltpu.get_barrier_semaphore()
    each_row(lambda q: pl.semaphore_signal(barrier, inc=1, device_id={"rows": q}, device_id_type=MESH))
    for off in range(1, 8):
        pl.semaphore_signal(
            barrier, inc=1, device_id={"leaf": lax.rem(leaf + off, 8)}, device_id_type=MESH
        )
    pl.semaphore_wait(barrier, 22)

    def send0(q):
        return rdma(p_ref.at[0, pl.ds(q * 32, 32)], share0.at[row], s0.at[q], r0.at[row], {"rows": q})

    def take0(q):
        return rdma(share0.at[q], share0.at[q], s0.at[q], r0.at[q], {"rows": q})

    each_row(lambda q: send0(q).start())

    def send_gram(q):
        return rdma(gram_ref.at[pl.ds(3, 3), pl.ds(q * 8, 8)], gparts.at[row], sg.at[q], rg.at[row], {"rows": q})

    def take_gram(q):
        return rdma(gparts.at[q], gparts.at[q], sg.at[q], rg.at[q], {"rows": q})

    each_row(lambda q: send_gram(q).start())
    share0[row] = p_ref[0, pl.ds(row * 32, 32)]
    gparts[row] = gram_ref[3:6, pl.ds(row * 8, 8)]
    each_row(lambda q: take0(q).wait_recv())
    low_child = share0[0]
    high_child = share0[8]
    for i in range(1, 8):
        low_child = low_child + share0[i]
        high_child = high_child + share0[8 + i]
    pair = jnp.concatenate([low_child, high_child], axis=1)
    c0 = mm3(pair, whi_ref[:, 0:256], wlo_ref[:, 0:256])
    mine0[0] = c0[:, 0:128]
    mine0[1] = c0[:, 128:256]

    def send_c0(q):
        return rdma(mine0.at[q // 8], coef.at[0, pl.ds(row * 32, 32)], sc.at[0, q], rc.at[0, row], {"rows": q})

    def take_c(level, q):
        spot = coef.at[level, pl.ds(q * 32, 32)]
        return rdma(spot, spot, sc.at[level, q], rc.at[level, q], {"rows": q})

    each_row(lambda q: send_c0(q).start())
    coef[0, pl.ds(row * 32, 32)] = mine0[row // 8]

    each_row(lambda q: take_gram(q).wait_recv())
    total = gparts[0]
    for i in range(1, 16):
        total = total + gparts[i]
    gsum[:, pl.ds(row * 8, 8)] = total

    def send_sum(q):
        spot = gsum.at[:, pl.ds(row * 8, 8)]
        return rdma(spot, spot, sga.at[q], rga.at[row], {"rows": q})

    def take_sum(q):
        spot = gsum.at[:, pl.ds(q * 8, 8)]
        return rdma(spot, spot, sga.at[q], rga.at[q], {"rows": q})

    each_row(lambda q: send_sum(q).start())

    each_row(lambda q: take_c(0, q).wait_recv())
    c0_hi, c0_lo = halves(coef[0])

    def send_rest(level, q):
        return rdma(
            rest.at[level - 1, pl.ds(q * 32, 32)], shares.at[level - 1, row],
            ss.at[level - 1, q], rs.at[level - 1, row], {"rows": q},
        )

    def take_rest(level, q):
        spot = shares.at[level - 1, q]
        return rdma(spot, spot, ss.at[level - 1, q], rs.at[level - 1, q], {"rows": q})

    for level in range(1, 4):
        g_hi, g_lo = halves(gram_ref[level - 1])
        rest[level - 1] = p_ref[level] - (mm(c0_hi, g_hi) + mm(c0_lo, g_hi) + mm(c0_hi, g_lo))
        each_row(lambda q: send_rest(level, q).start())
        shares[level - 1, row] = rest[level - 1, pl.ds(row * 32, 32)]

    def summed(level):
        each_row(lambda q: take_rest(level, q).wait_recv())
        value = shares[level - 1, 0]
        for i in range(1, 16):
            value = value + shares[level - 1, i]
        return value

    def round_up(level, buf, sems, remote, count, value):
        base, spot, peers = leaf_peers(count)
        buf[spot] = value
        for q in peers:
            rdma(buf.at[spot], buf.at[spot], sems.at[q], remote.at[spot], {"leaf": base + q}).start()
        for q in peers:
            rdma(buf.at[q], buf.at[q], sems.at[q], remote.at[q], {"leaf": base + q}).wait_recv()
        half = count // 2
        low, high = buf[0], buf[half]
        for i in range(1, half):
            low = low + buf[i]
            high = high + buf[half + i]
        cut = slice(128 + level * 128, 256 + level * 128)
        c = mm3(jnp.concatenate([low, high], axis=1), whi_ref[:, cut], wlo_ref[:, cut])
        coef[level, pl.ds(row * 32, 32)] = c

        def send_c(q):
            own = coef.at[level, pl.ds(row * 32, 32)]
            return rdma(own, own, sc.at[level, q], rc.at[level, row], {"rows": q})

        each_row(lambda q: send_c(q).start())
        return c

    c1 = round_up(1, pair1, se1, re1, 2, summed(1))
    each_row(lambda q: take_sum(q).wait_recv())
    g21 = halves(gsum[0])
    g31 = halves(gsum[1])
    g32 = halves(gsum[2])
    part2 = summed(2) - mm3(c1, *g21)
    part3 = summed(3) - mm3(c1, *g31)
    c2 = round_up(2, quad2, se2, re2, 4, part2)
    round_up(3, oct3, se3, re3, 8, part3 - mm3(c2, *g32))

    for level in range(4):
        if level > 0:
            each_row(lambda q: take_c(level, q).wait_recv())
        hi, lo = halves(-jnp.transpose(coef[level]))
        chi_ref[level * 128 : level * 128 + 128, :] = hi
        clo_ref[level * 128 : level * 128 + 128, :] = lo

    def sent(q):
        send0(q).wait_send()
        send_gram(q).wait_send()
        send_c0(q).wait_send()
        send_sum(q).wait_send()
        for level in range(1, 4):
            send_rest(level, q).wait_send()
            take_c(level, q).wait_send()

    each_row(sent)
    for buf, sems, remote, count in ((pair1, se1, re1, 2), (quad2, se2, re2, 4), (oct3, se3, re3, 8)):
        base, spot, peers = leaf_peers(count)
        for q in peers:
            rdma(buf.at[spot], buf.at[spot], sems.at[q], remote.at[spot], {"leaf": base + q}).wait_send()


def back_kernel(rhs_ref, order_ref, inv_ref, left_ref, chi_ref, clo_ref, out_ref):
    place = one_hot(order_ref[...], 256)
    moved = mm(inv_ref[...], place, NT).astype(BF16)
    total = mm(moved, rhs_ref[...])
    left = jnp.concatenate([left_ref[level] for level in range(4)], axis=1)
    out_ref[...] = total + mm(left, chi_ref[...]) + mm(left, clo_ref[...])


def per_device(rhs, leaf_order, leaf_inv, right_basis, left_basis, rank_perm, joined):
    blocks = leaf_inv.shape[0]
    leaf = lax.axis_index("leaf")
    order = leaf_order.reshape(blocks, 1, 256)
    node = jnp.stack(
        [leaf, 8 + leaf // 2, 12 + leaf // 4, 14 + 0 * leaf, leaf % 2, leaf // 2 % 2, leaf // 4 % 2]
    ).astype(jnp.int32)

    rhs_spec = pl.BlockSpec((256, 512), lambda b, *_: (b, 0))
    order_spec = pl.BlockSpec((None, 1, 256), lambda b, *_: (b, 0, 0))
    inv_spec = pl.BlockSpec((None, 256, 256), lambda b, *_: (b, 0, 0))
    basis_spec = pl.BlockSpec((4, 256, 128), lambda b, *_: (0, b, 0))

    def whole(*dims):
        return pl.BlockSpec(dims, lambda b, *_: (0,) * len(dims))

    def half_node(level):
        return pl.BlockSpec((None, 128, 256), lambda b, n: (n[level], n[3 + level], 0))

    p, gram, w_hi, w_lo = pl.pallas_call(
        front_kernel,
        out_shape=(
            jax.ShapeDtypeStruct((4, 512, 128), F32),
            jax.ShapeDtypeStruct((6, 128, 128), F32),
            jax.ShapeDtypeStruct((256, 640), BF16),
            jax.ShapeDtypeStruct((256, 640), BF16),
        ),
        grid_spec=pltpu.PrefetchScalarGridSpec(
            num_scalar_prefetch=1,
            grid=(blocks,),
            in_specs=[
                rhs_spec, order_spec, inv_spec, basis_spec, basis_spec, whole(4, 128),
                pl.BlockSpec((None, 256, 256), lambda b, n: (n[0], 0, 0)),
                half_node(1), half_node(2), half_node(3),
            ],
            out_specs=(whole(4, 512, 128), whole(6, 128, 128), whole(256, 640), whole(256, 640)),
        ),
        compiler_params=pltpu.CompilerParams(
            dimension_semantics=("arbitrary",), vmem_limit_bytes=VMEM_LIMIT
        ),
        name="front",
    )(node, rhs, order, leaf_inv, right_basis, left_basis, rank_perm, joined, joined, joined, joined)

    dma = pltpu.SemaphoreType.DMA
    vmem = pl.BlockSpec(memory_space=pltpu.VMEM)
    c_hi, c_lo = pl.pallas_call(
        exchange_kernel,
        out_shape=(jax.ShapeDtypeStruct((512, 512), BF16), jax.ShapeDtypeStruct((512, 512), BF16)),
        in_specs=[vmem] * 4,
        out_specs=(vmem, vmem),
        scratch_shapes=[
            pltpu.VMEM((4, 512, 128), F32),
            pltpu.VMEM((16, 32, 128), F32),
            pltpu.VMEM((3, 16, 32, 128), F32),
            pltpu.VMEM((3, 512, 128), F32),
            pltpu.VMEM((2, 32, 128), F32),
            pltpu.VMEM((16, 3, 8, 128), F32),
            pltpu.VMEM((3, 128, 128), F32),
            pltpu.VMEM((2, 32, 128), F32),
            pltpu.VMEM((4, 32, 128), F32),
            pltpu.VMEM((8, 32, 128), F32),
            dma((16,)), dma((16,)), dma((16,)), dma((16,)), dma((16,)), dma((16,)),
            dma((3, 16)), dma((3, 16)), dma((4, 16)), dma((4, 16)),
            dma((2,)), dma((2,)), dma((4,)), dma((4,)), dma((8,)), dma((8,)),
        ],
        compiler_params=pltpu.CompilerParams(
            collective_id=0, has_side_effects=True, vmem_limit_bytes=VMEM_LIMIT
        ),
        name="exchange",
    )(p, gram, w_hi, w_lo)

    return pl.pallas_call(
        back_kernel,
        out_shape=jax.ShapeDtypeStruct(rhs.shape, F32),
        grid=(blocks,),
        in_specs=[rhs_spec, order_spec, inv_spec, basis_spec, whole(512, 512), whole(512, 512)],
        out_specs=pl.BlockSpec((256, 512), lambda b: (b, 0)),
        compiler_params=pltpu.CompilerParams(
            dimension_semantics=("arbitrary",), vmem_limit_bytes=VMEM_LIMIT
        ),
        name="back",
    )(rhs, order, leaf_inv, left_basis, c_hi, c_lo)


def solution(mesh):
    return jax.shard_map(
        per_device,
        mesh=mesh,
        in_specs=(
            P(("leaf", "rows"), None),
            P(("leaf", "rows"), None),
            P(("leaf", "rows"), None, None),
            P(None, ("leaf", "rows"), None),
            P(None, ("leaf", "rows"), None),
            P(),
            P(),
        ),
        out_specs=P(("leaf", "rows"), None),
        check_vma=False,
    )
```

```python
import jax
import jax.numpy as jnp
from jax import lax
from jax.experimental import pallas as pl
from jax.experimental.pallas import tpu as pltpu
from jax.sharding import PartitionSpec as P

F32 = jnp.float32
BF16 = jnp.bfloat16
MESH = pl.DeviceIdType.MESH
TN = (((0,), (0,)), ((), ()))
NT = (((1,), (1,)), ((), ()))
NN = (((1,), (0,)), ((), ()))
CHUNKS = 6
PER = 3
CHUNK = 256 * PER


def mm(a, b, dims=NN):
    return lax.dot_general(a, b, dims, preferred_element_type=F32)


def halves(x):
    hi = x.astype(BF16)
    return hi, (x - hi.astype(F32)).astype(BF16)


def side_by_side(x):
    return jnp.concatenate(halves(x), axis=1)


def mm3(x, w_hi, w_lo):
    hi, lo = halves(x)
    return mm(hi, w_hi) + mm(lo, w_hi) + mm(hi, w_lo)


def one_hot(row, count):
    width = row.shape[1]
    spot = lax.broadcasted_iota(jnp.int32, (count, width), 0)
    return jnp.where(spot == jnp.broadcast_to(row, (count, width)), 1.0, 0.0).astype(BF16)


def rdma(src, dst, ssem, rsem, where):
    return pltpu.make_async_remote_copy(
        src_ref=src, dst_ref=dst, send_sem=ssem, recv_sem=rsem, device_id=where, device_id_type=MESH
    )


def main_kernel(
    rhs_hbm, order_ref, inv_hbm, right_hbm, left_hbm, perm_ref, joined_hbm, cur_hbm, last_ref,
    rhs, inv, right, left, cur, node0, nodes, w_hi, w_lo, pairs, gram,
    coef, share0, shares, rest, mine0, gparts, gsum, pair1, quad2, oct3,
    rhs_sem, inv_sem, right_sem, rest_sem, left_sem, node_sem, out_sem,
    s0, r0, sg, rg, sga, rga, ss, rs, sc, rc, se, re,
):
    leaf = lax.axis_index("leaf")
    row = lax.axis_index("rows")
    near = {"rows": lax.rem(row + 1, 16)}

    def rows_of(chunk):
        return pl.ds(pl.multiple_of(chunk * CHUNK, CHUNK), CHUNK)

    def load(chunk):
        spot = rows_of(chunk)
        blocks = pl.ds(chunk * PER, PER)
        return (
            pltpu.make_async_copy(rhs_hbm.at[spot], rhs.at[spot], rhs_sem.at[chunk]),
            pltpu.make_async_copy(inv_hbm.at[blocks], inv.at[blocks], inv_sem.at[chunk]),
            pltpu.make_async_copy(
                right_hbm.at[pl.ds(0, 2), spot], right.at[pl.ds(0, 2), spot], right_sem.at[chunk]
            ),
        )

    for chunk in range(CHUNKS):
        for copy in load(chunk):
            copy.start()
    left_copy = pltpu.make_async_copy(left_hbm.at[pl.ds(0, 3)], left, left_sem)
    rest_copy = pltpu.make_async_copy(right_hbm.at[pl.ds(2, 2)], right.at[pl.ds(2, 2)], rest_sem)
    left_copy.start()
    rest_copy.start()
    node_copies = [pltpu.make_async_copy(joined_hbm.at[leaf], node0, node_sem.at[0])]
    for level in range(1, 4):
        node = 16 - 16 // 2**level + leaf // 2**level
        side = leaf // 2 ** (level - 1) % 2
        node_copies.append(
            pltpu.make_async_copy(
                joined_hbm.at[node, pl.ds(side * 128, 128)], nodes.at[level - 1], node_sem.at[level]
            )
        )
    for copy in node_copies:
        copy.start()

    def each_row(body):
        def step(off, carry):
            body(lax.rem(row + off, 16))
            return carry

        lax.fori_loop(1, 16, step, 0)

    barrier = pltpu.get_barrier_semaphore()
    each_row(lambda q: pl.semaphore_signal(barrier, inc=1, device_id={"rows": q}, device_id_type=MESH))
    for off in range(1, 8):
        pl.semaphore_signal(
            barrier, inc=1, device_id={"leaf": lax.rem(leaf + off, 8)}, device_id_type=MESH
        )

    def project(chunk, pair):
        spot = rows_of(chunk)
        hi, lo = halves(cur[spot, :])
        basis = jnp.concatenate([right[2 * pair, spot, :], right[2 * pair + 1, spot, :]], axis=1)
        pairs[pair] += mm(hi, basis, TN) + mm(lo, basis, TN)

    pairs[...] = jnp.zeros_like(pairs)
    gram[...] = jnp.zeros_like(gram)

    def solve_leaves(chunk, carry):
        for copy in load(chunk):
            copy.wait()
        for i in range(PER):
            block = chunk * PER + i
            spot = pl.ds(pl.multiple_of(block * 256, 256), 256)
            moved = mm(inv[block], one_hot(order_ref[block], 256), NT).astype(BF16)
            cur[spot, :] = mm(moved, rhs[spot, :])
        project(chunk, 0)
        return carry

    lax.fori_loop(0, CHUNKS, solve_leaves, 0)

    pl.semaphore_wait(barrier, 22)

    def send0(q):
        src = pairs.at[0, pl.ds(q * 32, 32), pl.ds(0, 128)]
        return rdma(src, share0.at[row], s0, r0, {"rows": q})

    each_row(lambda q: send0(q).start())
    share0[row] = pairs[0, pl.ds(row * 32, 32), 0:128]
    all0 = share0.at[pl.ds(0, 15)]

    left_copy.wait()
    rest_copy.wait()

    def multiply(chunk, carry):
        spot = rows_of(chunk)
        basis = [right[level, spot, :] for level in range(1, 4)]
        for low in range(3):
            gram[low, :, low * 128 :] += mm(left[low, spot, :], jnp.concatenate(basis[low:], axis=1), TN)
        return carry

    lax.fori_loop(0, CHUNKS, multiply, 0)

    def send_gram(q):
        return rdma(gram.at[pl.ds(1, 2), pl.ds(q * 8, 8)], gparts.at[row], sg, rg, {"rows": q})

    each_row(lambda q: send_gram(q).start())
    gparts[row] = gram[1:3, pl.ds(row * 8, 8), :]

    def project_rest(chunk, carry):
        project(chunk, 1)
        return carry

    lax.fori_loop(0, CHUNKS, project_rest, 0)

    for copy in node_copies:
        copy.wait()
    start = 0
    for level in range(4):
        hot = one_hot(perm_ref[level : level + 1, :], 128)
        hi, lo = halves(node0[...] if level == 0 else nodes[level - 1])
        count = hi.shape[0]
        for side in range(2):
            cut = slice(side * 128, side * 128 + 128)
            w_hi[cut, start : start + count] = mm(hot, hi[:, cut], NT).astype(BF16)
            w_lo[cut, start : start + count] = mm(hot, lo[:, cut], NT).astype(BF16)
        start += count

    rdma(all0, all0, s0, r0, near).wait_recv()
    low_child = share0[0]
    high_child = share0[8]
    for i in range(1, 8):
        low_child = low_child + share0[i]
        high_child = high_child + share0[8 + i]
    c0 = mm3(jnp.concatenate([low_child, high_child], axis=1), w_hi[:, 0:256], w_lo[:, 0:256])
    mine0[0] = c0[:, 0:128]
    mine0[1] = c0[:, 128:256]
    own = pl.ds(row * 32, 32)

    def send_c0(q):
        return rdma(mine0.at[q // 8], coef.at[0, own], sc.at[0], rc.at[0], {"rows": q})

    each_row(lambda q: send_c0(q).start())
    coef[0, own] = mine0[row // 8]

    def gathered(level):
        spot = coef.at[level, pl.ds(0, 480)]
        rdma(spot, spot, sc.at[level], rc.at[level], near).wait_recv()

    all_parts = gparts.at[pl.ds(0, 15)]
    rdma(all_parts, all_parts, sg, rg, near).wait_recv()
    total = gparts[0]
    for i in range(1, 16):
        total = total + gparts[i]
    own8 = pl.ds(row * 8, 8)
    gsum[:, own8] = total

    def send_sum(q):
        return rdma(gsum.at[:, own8], gsum.at[:, own8], sga, rga, {"rows": q})

    each_row(lambda q: send_sum(q).start())

    gathered(0)
    c0_hi, c0_lo = halves(coef[0])

    def send_rest(level, q):
        return rdma(
            rest.at[level - 1, pl.ds(q * 32, 32)], shares.at[level - 1, row],
            ss.at[level - 1], rs.at[level - 1], {"rows": q},
        )

    for level in range(1, 4):
        lanes = slice(level * 128 - 128, level * 128)
        g_hi, g_lo = halves(gram[0, :, lanes])
        half = slice(level % 2 * 128, level % 2 * 128 + 128)
        taken = mm(c0_hi, g_hi) + mm(c0_lo, g_hi) + mm(c0_hi, g_lo)
        rest[level - 1] = pairs[level // 2, :, half] - taken
        each_row(lambda q: send_rest(level, q).start())
        shares[level - 1, row] = rest[level - 1, own]

    first = jnp.concatenate([c0_hi, c0_lo], axis=1)

    def correct_first(chunk, carry):
        spot = rows_of(chunk)
        basis = left[0, spot, :]
        cur[spot, :] = cur[spot, :] - mm(jnp.concatenate([basis, basis], axis=1), first, NT)
        return carry

    lax.fori_loop(0, CHUNKS, correct_first, 0)

    def summed(level):
        spot = shares.at[level - 1, pl.ds(0, 15)]
        rdma(spot, spot, ss.at[level - 1], rs.at[level - 1], near).wait_recv()
        value = shares[level - 1, 0]
        for i in range(1, 16):
            value = value + shares[level - 1, i]
        return value

    def up_sends(level, buf):
        count = 2**level
        base = leaf // count * count
        spot = leaf - base
        return [
            rdma(
                buf.at[spot], buf.at[spot], se.at[level - 1], re.at[level - 1],
                {"leaf": base + lax.rem(spot + off, count)},
            )
            for off in range(1, count)
        ]

    def up(level, buf, value):
        count = 2**level
        buf[leaf % count] = value
        sends = up_sends(level, buf)
        for copy in sends:
            copy.start()
        spot = buf.at[pl.ds(0, count - 1)]
        rdma(spot, spot, se.at[level - 1], re.at[level - 1], near).wait_recv()
        half = count // 2
        low, high = buf[0], buf[half]
        for i in range(1, half):
            low = low + buf[i]
            high = high + buf[half + i]
        cut = slice(128 + level * 128, 256 + level * 128)
        c = mm3(jnp.concatenate([low, high], axis=1), w_hi[:, cut], w_lo[:, cut])
        coef[level, own] = c
        each_row(lambda q: send_c(level, q).start())
        return c

    def send_c(level, q):
        return rdma(coef.at[level, own], coef.at[level, own], sc.at[level], rc.at[level], {"rows": q})

    c1 = up(1, pair1, summed(1))
    spot = gsum.at[:, pl.ds(0, 120)]
    rdma(spot, spot, sga, rga, near).wait_recv()
    part2 = summed(2) - mm3(c1, *halves(gsum[0, :, 128:256]))
    part3 = summed(3) - mm3(c1, *halves(gsum[0, :, 256:384]))
    c2 = up(2, quad2, part2)
    up(3, oct3, part3 - mm3(c2, *halves(gsum[1, :, 256:384])))

    gathered(1)
    gathered(2)
    middle = jnp.concatenate([side_by_side(coef[1]), side_by_side(coef[2])], axis=1)

    def store(chunk):
        spot = rows_of(chunk)
        return pltpu.make_async_copy(cur.at[spot], cur_hbm.at[spot], out_sem.at[chunk])

    def correct_middle(chunk, carry):
        spot = rows_of(chunk)
        one, two = left[1, spot, :], left[2, spot, :]
        cur[spot, :] = cur[spot, :] - mm(jnp.concatenate([one, one, two, two], axis=1), middle, NT)
        store(chunk).start()
        return carry

    lax.fori_loop(0, CHUNKS, correct_middle, 0)
    gathered(3)
    last_ref[...] = side_by_side(coef[3])

    rdma(all0, all0, s0, r0, near).wait_send()
    rdma(all_parts, all_parts, sg, rg, near).wait_send()
    rdma(spot, spot, sga, rga, near).wait_send()
    for level in range(4):
        span = coef.at[level, pl.ds(0, 480)]
        rdma(span, span, sc.at[level], rc.at[level], near).wait_send()
    for level in range(1, 4):
        span = shares.at[level - 1, pl.ds(0, 15)]
        rdma(span, span, ss.at[level - 1], rs.at[level - 1], near).wait_send()
    for level, buf in ((1, pair1), (2, quad2), (3, oct3)):
        span = buf.at[pl.ds(0, 2**level - 1)]
        rdma(span, span, se.at[level - 1], re.at[level - 1], near).wait_send()
    for chunk in range(CHUNKS):
        store(chunk).wait()


def last_kernel(cur_ref, left_ref, last_ref, out_ref):
    basis = left_ref[...]
    out_ref[...] = cur_ref[...] - mm(jnp.concatenate([basis, basis], axis=1), last_ref[...], NT)


def per_device(rhs, leaf_order, leaf_inv, right_basis, left_basis, rank_perm, joined):
    blocks = leaf_inv.shape[0]
    order = leaf_order.reshape(blocks, 1, 256)
    count = rhs.shape[0]
    dma = pltpu.SemaphoreType.DMA
    vmem = pl.BlockSpec(memory_space=pltpu.VMEM)
    hbm = pl.BlockSpec(memory_space=pl.ANY)
    cur, last = pl.pallas_call(
        main_kernel,
        out_shape=(jax.ShapeDtypeStruct(rhs.shape, F32), jax.ShapeDtypeStruct((512, 256), BF16)),
        in_specs=[hbm, vmem, hbm, hbm, hbm, vmem, hbm],
        out_specs=(hbm, vmem),
        scratch_shapes=[
            pltpu.VMEM((count, 512), BF16),
            pltpu.VMEM((blocks, 256, 256), BF16),
            pltpu.VMEM((4, count, 128), BF16),
            pltpu.VMEM((3, count, 128), BF16),
            pltpu.VMEM((count, 512), F32),
            pltpu.VMEM((256, 256), F32),
            pltpu.VMEM((3, 128, 256), F32),
            pltpu.VMEM((256, 640), BF16),
            pltpu.VMEM((256, 640), BF16),
            pltpu.VMEM((2, 512, 256), F32),
            pltpu.VMEM((3, 128, 384), F32),
            pltpu.VMEM((4, 512, 128), F32),
            pltpu.VMEM((16, 32, 128), F32),
            pltpu.VMEM((3, 16, 32, 128), F32),
            pltpu.VMEM((3, 512, 128), F32),
            pltpu.VMEM((2, 32, 128), F32),
            pltpu.VMEM((16, 2, 8, 384), F32),
            pltpu.VMEM((2, 128, 384), F32),
            pltpu.VMEM((2, 32, 128), F32),
            pltpu.VMEM((4, 32, 128), F32),
            pltpu.VMEM((8, 32, 128), F32),
            dma((CHUNKS,)), dma((CHUNKS,)), dma((CHUNKS,)), dma, dma, dma((4,)), dma((CHUNKS,)),
            dma, dma, dma, dma, dma, dma, dma((3,)), dma((3,)), dma((4,)), dma((4,)), dma((3,)), dma((3,)),
        ],
        compiler_params=pltpu.CompilerParams(
            collective_id=0, has_side_effects=True, vmem_limit_bytes=56 * 1024 * 1024
        ),
        name="main",
    )(rhs, order, leaf_inv, right_basis, left_basis, rank_perm, joined)

    tile = 512
    return pl.pallas_call(
        last_kernel,
        out_shape=jax.ShapeDtypeStruct(rhs.shape, F32),
        grid=(count // tile,),
        in_specs=[
            pl.BlockSpec((tile, 512), lambda b: (b, 0)),
            pl.BlockSpec((None, tile, 128), lambda b: (3, b, 0)),
            pl.BlockSpec((512, 256), lambda b: (0, 0)),
        ],
        out_specs=pl.BlockSpec((tile, 512), lambda b: (b, 0)),
        compiler_params=pltpu.CompilerParams(
            dimension_semantics=("arbitrary",), vmem_limit_bytes=32 * 1024 * 1024
        ),
        name="last",
    )(cur, left_basis, last)


def solution(mesh):
    return jax.shard_map(
        per_device,
        mesh=mesh,
        in_specs=(
            P(("leaf", "rows"), None),
            P(("leaf", "rows"), None),
            P(("leaf", "rows"), None, None),
            P(None, ("leaf", "rows"), None),
            P(None, ("leaf", "rows"), None),
            P(),
            P(),
        ),
        out_specs=P(("leaf", "rows"), None),
        check_vma=False,
    )
```

```python
import jax
import jax.numpy as jnp
from jax import lax
from jax.experimental import pallas as pl
from jax.experimental.pallas import tpu as pltpu
from jax.sharding import PartitionSpec as P

F32 = jnp.float32
BF16 = jnp.bfloat16
MESH = pl.DeviceIdType.MESH
TN = (((0,), (0,)), ((), ()))
NT = (((1,), (1,)), ((), ()))
NN = (((1,), (0,)), ((), ()))
CHUNKS = 6
PER = 3
CHUNK = 256 * PER


def mm(a, b, dims=NN):
    return lax.dot_general(a, b, dims, preferred_element_type=F32)


def halves(x):
    hi = x.astype(BF16)
    return hi, (x - hi.astype(F32)).astype(BF16)


def side_by_side(x):
    return jnp.concatenate(halves(x), axis=1)


def mm3(x, w_hi, w_lo):
    hi, lo = halves(x)
    return mm(hi, w_hi) + mm(lo, w_hi) + mm(hi, w_lo)


def one_hot(row, count):
    width = row.shape[1]
    spot = lax.broadcasted_iota(jnp.int32, (count, width), 0)
    return jnp.where(spot == jnp.broadcast_to(row, (count, width)), 1.0, 0.0).astype(BF16)


def rdma(src, dst, ssem, rsem, where):
    return pltpu.make_async_remote_copy(
        src_ref=src, dst_ref=dst, send_sem=ssem, recv_sem=rsem, device_id=where, device_id_type=MESH
    )


def main_kernel(
    rhs_hbm, order_ref, inv_hbm, right_hbm, left_hbm, perm_ref, joined_hbm, cur_hbm, last_ref,
    rhs, inv, right, left, cur, folded, turned, node0, nodes, w_hi, w_lo, pairs, gram,
    coef, share0, shares, rest, mine0, gparts, gsum, pair1, quad2, oct3,
    rhs_sem, inv_sem, right_sem, rest_sem, left_sem, node_sem, out_sem,
    s0, r0, sg, rg, sga, rga, ss, rs, sc, rc, se, re,
):
    leaf = lax.axis_index("leaf")
    row = lax.axis_index("rows")
    near = {"rows": lax.rem(row + 1, 16)}

    def rows_of(chunk):
        return pl.ds(pl.multiple_of(chunk * CHUNK, CHUNK), CHUNK)

    def load(chunk):
        spot = rows_of(chunk)
        blocks = pl.ds(chunk * PER, PER)
        return (
            pltpu.make_async_copy(rhs_hbm.at[spot], rhs.at[spot], rhs_sem.at[chunk]),
            pltpu.make_async_copy(inv_hbm.at[blocks], inv.at[blocks], inv_sem.at[chunk]),
            pltpu.make_async_copy(
                right_hbm.at[pl.ds(0, 2), spot], right.at[pl.ds(0, 2), spot], right_sem.at[chunk]
            ),
        )

    for chunk in range(CHUNKS):
        for copy in load(chunk):
            copy.start()
    left_copy = pltpu.make_async_copy(left_hbm.at[pl.ds(0, 3)], left, left_sem)
    rest_copy = pltpu.make_async_copy(right_hbm.at[pl.ds(2, 2)], right.at[pl.ds(2, 2)], rest_sem)
    left_copy.start()
    rest_copy.start()
    node_copies = [pltpu.make_async_copy(joined_hbm.at[leaf], node0, node_sem.at[0])]
    for level in range(1, 4):
        node = 16 - 16 // 2**level + leaf // 2**level
        side = leaf // 2 ** (level - 1) % 2
        node_copies.append(
            pltpu.make_async_copy(
                joined_hbm.at[node, pl.ds(side * 128, 128)], nodes.at[level - 1], node_sem.at[level]
            )
        )
    for copy in node_copies:
        copy.start()

    def each_row(body):
        for off in range(1, 16):
            body(lax.rem(row + off, 16))

    barrier = pltpu.get_barrier_semaphore()
    each_row(lambda q: pl.semaphore_signal(barrier, inc=1, device_id={"rows": q}, device_id_type=MESH))
    for off in range(1, 8):
        pl.semaphore_signal(
            barrier, inc=1, device_id={"leaf": lax.rem(leaf + off, 8)}, device_id_type=MESH
        )

    def solve_leaves(chunk):
        for i in range(PER):
            block = chunk * PER + i
            spot = slice(block * 256, block * 256 + 256)
            moved = mm(one_hot(order_ref[block : block + 1, :], 256), inv[block], NT).astype(BF16)
            inv[block] = moved
            basis = jnp.concatenate([right[0, spot, :], right[1, spot, :]], axis=1)
            hi, lo = halves(mm(moved, basis))
            part = slice(i * 256, i * 256 + 256)
            folded[chunk % 2, 0, part, :] = hi
            folded[chunk % 2, 1, part, :] = lo
        turned[chunk] = jnp.transpose(rhs[chunk * CHUNK : chunk * CHUNK + CHUNK, :])

    def project_first(chunk):
        cols = turned[chunk]
        terms = mm(cols, folded[chunk % 2, 0]) + mm(cols, folded[chunk % 2, 1])
        pairs[0] = terms if chunk == 0 else pairs[0] + terms

    for chunk in range(CHUNKS):
        for copy in load(chunk):
            copy.wait()
        if chunk > 0:
            project_first(chunk - 1)
        solve_leaves(chunk)
    project_first(CHUNKS - 1)

    pl.semaphore_wait(barrier, 22)

    def send0(q):
        src = pairs.at[0, pl.ds(q * 32, 32), pl.ds(0, 128)]
        return rdma(src, share0.at[row], s0, r0, {"rows": q})

    each_row(lambda q: send0(q).start())
    share0[row] = pairs[0, pl.ds(row * 32, 32), 0:128]
    all0 = share0.at[pl.ds(0, 15)]

    left_copy.wait()
    rest_copy.wait()
    gram[...] = jnp.zeros_like(gram)
    pairs[1] = jnp.zeros_like(pairs[1])

    def multiply(chunk, carry):
        spot = rows_of(chunk)
        basis = [right[level, spot, :] for level in range(1, 4)]
        for low in range(3):
            gram[low, :, low * 128 :] += mm(left[low, spot, :], jnp.concatenate(basis[low:], axis=1), TN)
        return carry

    lax.fori_loop(0, CHUNKS, multiply, 0)

    def send_gram(q):
        return rdma(gram.at[pl.ds(1, 2), pl.ds(q * 8, 8)], gparts.at[row], sg, rg, {"rows": q})

    each_row(lambda q: send_gram(q).start())
    gparts[row] = gram[1:3, pl.ds(row * 8, 8), :]

    for copy in node_copies:
        copy.wait()
    start = 0
    for level in range(4):
        hot = one_hot(perm_ref[level : level + 1, :], 128)
        hi, lo = halves(node0[...] if level == 0 else nodes[level - 1])
        count = hi.shape[0]
        for side in range(2):
            cut = slice(side * 128, side * 128 + 128)
            w_hi[cut, start : start + count] = mm(hot, hi[:, cut], NT).astype(BF16)
            w_lo[cut, start : start + count] = mm(hot, lo[:, cut], NT).astype(BF16)
        start += count

    rdma(all0, all0, s0, r0, near).wait_recv()
    low_child = share0[0]
    high_child = share0[8]
    for i in range(1, 8):
        low_child = low_child + share0[i]
        high_child = high_child + share0[8 + i]
    c0 = mm3(jnp.concatenate([low_child, high_child], axis=1), w_hi[:, 0:256], w_lo[:, 0:256])
    mine0[0] = c0[:, 0:128]
    mine0[1] = c0[:, 128:256]
    own = pl.ds(row * 32, 32)

    def send_c0(q):
        return rdma(mine0.at[q // 8], coef.at[0, own], sc.at[0], rc.at[0], {"rows": q})

    each_row(lambda q: send_c0(q).start())
    coef[0, own] = mine0[row // 8]

    def gathered(level):
        spot = coef.at[level, pl.ds(0, 480)]
        rdma(spot, spot, sc.at[level], rc.at[level], near).wait_recv()

    all_parts = gparts.at[pl.ds(0, 15)]
    rdma(all_parts, all_parts, sg, rg, near).wait_recv()
    total = gparts[0]
    for i in range(1, 16):
        total = total + gparts[i]
    own8 = pl.ds(row * 8, 8)
    gsum[:, own8] = total

    def send_sum(q):
        return rdma(gsum.at[:, own8], gsum.at[:, own8], sga, rga, {"rows": q})

    each_row(lambda q: send_sum(q).start())

    def project_rest(chunk, carry):
        parts = []
        for i in range(PER):
            spot = pl.ds(pl.multiple_of(chunk * CHUNK + i * 256, 256), 256)
            basis = jnp.concatenate([right[2, spot, :], right[3, spot, :]], axis=1)
            parts.append(halves(mm(inv[chunk * PER + i], basis)))
        cols = turned[chunk]
        hi = jnp.concatenate([part[0] for part in parts], axis=0)
        lo = jnp.concatenate([part[1] for part in parts], axis=0)
        pairs[1] += mm(cols, hi) + mm(cols, lo)
        return carry

    lax.fori_loop(0, CHUNKS, project_rest, 0)

    gathered(0)
    c0_hi, c0_lo = halves(coef[0])

    def send_rest(level, q):
        return rdma(
            rest.at[level - 1, pl.ds(q * 32, 32)], shares.at[level - 1, row],
            ss.at[level - 1], rs.at[level - 1], {"rows": q},
        )

    for level in range(1, 4):
        lanes = slice(level * 128 - 128, level * 128)
        g_hi, g_lo = halves(gram[0, :, lanes])
        half = slice(level % 2 * 128, level % 2 * 128 + 128)
        taken = mm(c0_hi, g_hi) + mm(c0_lo, g_hi) + mm(c0_hi, g_lo)
        rest[level - 1] = pairs[level // 2, :, half] - taken
        each_row(lambda q: send_rest(level, q).start())
        shares[level - 1, row] = rest[level - 1, own]

    first = jnp.concatenate([c0_hi, c0_lo], axis=1)

    def correct_first(chunk, carry):
        for i in range(PER):
            spot = pl.ds(pl.multiple_of(chunk * CHUNK + i * 256, 256), 256)
            basis = left[0, spot, :]
            taken = mm(jnp.concatenate([basis, basis], axis=1), first, NT)
            cur[spot, :] = mm(inv[chunk * PER + i], rhs[spot, :], TN) - taken
        return carry

    lax.fori_loop(0, CHUNKS, correct_first, 0)

    def summed(level):
        spot = shares.at[level - 1, pl.ds(0, 15)]
        rdma(spot, spot, ss.at[level - 1], rs.at[level - 1], near).wait_recv()
        value = shares[level - 1, 0]
        for i in range(1, 16):
            value = value + shares[level - 1, i]
        return value

    def up_sends(level, buf):
        count = 2**level
        base = leaf // count * count
        spot = leaf - base
        return [
            rdma(
                buf.at[spot], buf.at[spot], se.at[level - 1], re.at[level - 1],
                {"leaf": base + lax.rem(spot + off, count)},
            )
            for off in range(1, count)
        ]

    def begin(level, buf, value):
        buf[leaf % 2**level] = value
        for copy in up_sends(level, buf):
            copy.start()

    def finish(level, buf):
        count = 2**level
        spot = buf.at[pl.ds(0, count - 1)]
        rdma(spot, spot, se.at[level - 1], re.at[level - 1], near).wait_recv()
        half = count // 2
        low, high = buf[0], buf[half]
        for i in range(1, half):
            low = low + buf[i]
            high = high + buf[half + i]
        cut = slice(128 + level * 128, 256 + level * 128)
        c = mm3(jnp.concatenate([low, high], axis=1), w_hi[:, cut], w_lo[:, cut])
        coef[level, own] = c
        return c

    def send_c(level, q):
        return rdma(coef.at[level, own], coef.at[level, own], sc.at[level], rc.at[level], {"rows": q})

    begin(1, pair1, summed(1))
    sums = gsum.at[:, pl.ds(0, 120)]
    rdma(sums, sums, sga, rga, near).wait_recv()
    g21 = halves(gsum[0, :, 128:256])
    g31 = halves(gsum[0, :, 256:384])
    g32 = halves(gsum[1, :, 256:384])
    part2 = summed(2)
    part3 = summed(3)
    c1 = finish(1, pair1)
    begin(2, quad2, part2 - mm3(c1, *g21))
    each_row(lambda q: send_c(1, q).start())
    part3 = part3 - mm3(c1, *g31)
    c2 = finish(2, quad2)
    begin(3, oct3, part3 - mm3(c2, *g32))
    each_row(lambda q: send_c(2, q).start())
    finish(3, oct3)
    each_row(lambda q: send_c(3, q).start())

    gathered(1)
    gathered(2)
    middle = jnp.concatenate([side_by_side(coef[1]), side_by_side(coef[2])], axis=1)

    def store(chunk):
        spot = rows_of(chunk)
        return pltpu.make_async_copy(cur.at[spot], cur_hbm.at[spot], out_sem.at[chunk])

    def correct_middle(chunk, carry):
        spot = rows_of(chunk)
        one, two = left[1, spot, :], left[2, spot, :]
        cur[spot, :] = cur[spot, :] - mm(jnp.concatenate([one, one, two, two], axis=1), middle, NT)
        store(chunk).start()
        return carry

    lax.fori_loop(0, CHUNKS, correct_middle, 0)
    gathered(3)
    last_ref[...] = side_by_side(coef[3])

    rdma(all0, all0, s0, r0, near).wait_send()
    rdma(all_parts, all_parts, sg, rg, near).wait_send()
    rdma(sums, sums, sga, rga, near).wait_send()
    for level in range(4):
        span = coef.at[level, pl.ds(0, 480)]
        rdma(span, span, sc.at[level], rc.at[level], near).wait_send()
    for level in range(1, 4):
        span = shares.at[level - 1, pl.ds(0, 15)]
        rdma(span, span, ss.at[level - 1], rs.at[level - 1], near).wait_send()
    for level, buf in ((1, pair1), (2, quad2), (3, oct3)):
        span = buf.at[pl.ds(0, 2**level - 1)]
        rdma(span, span, se.at[level - 1], re.at[level - 1], near).wait_send()
    for chunk in range(CHUNKS):
        store(chunk).wait()


def last_kernel(cur_ref, left_ref, last_ref, out_ref):
    basis = left_ref[...]
    out_ref[...] = cur_ref[...] - mm(jnp.concatenate([basis, basis], axis=1), last_ref[...], NT)


def per_device(rhs, leaf_order, leaf_inv, right_basis, left_basis, rank_perm, joined):
    blocks = leaf_inv.shape[0]
    count = rhs.shape[0]
    dma = pltpu.SemaphoreType.DMA
    vmem = pl.BlockSpec(memory_space=pltpu.VMEM)
    hbm = pl.BlockSpec(memory_space=pl.ANY)
    cur, last = pl.pallas_call(
        main_kernel,
        out_shape=(jax.ShapeDtypeStruct(rhs.shape, F32), jax.ShapeDtypeStruct((512, 256), BF16)),
        in_specs=[hbm, vmem, hbm, hbm, hbm, vmem, hbm],
        out_specs=(hbm, vmem),
        scratch_shapes=[
            pltpu.VMEM((count, 512), BF16),
            pltpu.VMEM((blocks, 256, 256), BF16),
            pltpu.VMEM((4, count, 128), BF16),
            pltpu.VMEM((3, count, 128), BF16),
            pltpu.VMEM((count, 512), F32),
            pltpu.VMEM((2, 2, CHUNK, 256), BF16),
            pltpu.VMEM((CHUNKS, 512, CHUNK), BF16),
            pltpu.VMEM((256, 256), F32),
            pltpu.VMEM((3, 128, 256), F32),
            pltpu.VMEM((256, 640), BF16),
            pltpu.VMEM((256, 640), BF16),
            pltpu.VMEM((2, 512, 256), F32),
            pltpu.VMEM((3, 128, 384), F32),
            pltpu.VMEM((4, 512, 128), F32),
            pltpu.VMEM((16, 32, 128), F32),
            pltpu.VMEM((3, 16, 32, 128), F32),
            pltpu.VMEM((3, 512, 128), F32),
            pltpu.VMEM((2, 32, 128), F32),
            pltpu.VMEM((16, 2, 8, 384), F32),
            pltpu.VMEM((2, 128, 384), F32),
            pltpu.VMEM((2, 32, 128), F32),
            pltpu.VMEM((4, 32, 128), F32),
            pltpu.VMEM((8, 32, 128), F32),
            dma((CHUNKS,)), dma((CHUNKS,)), dma((CHUNKS,)), dma, dma, dma((4,)), dma((CHUNKS,)),
            dma, dma, dma, dma, dma, dma, dma((3,)), dma((3,)), dma((4,)), dma((4,)), dma((3,)), dma((3,)),
        ],
        compiler_params=pltpu.CompilerParams(
            collective_id=0, has_side_effects=True, vmem_limit_bytes=56 * 1024 * 1024
        ),
        name="main",
    )(rhs, leaf_order, leaf_inv, right_basis, left_basis, rank_perm, joined)

    tile = 768
    return pl.pallas_call(
        last_kernel,
        out_shape=jax.ShapeDtypeStruct(rhs.shape, F32),
        grid=(count // tile,),
        in_specs=[
            pl.BlockSpec((tile, 512), lambda b: (b, 0)),
            pl.BlockSpec((None, tile, 128), lambda b: (3, b, 0)),
            pl.BlockSpec((512, 256), lambda b: (0, 0)),
        ],
        out_specs=pl.BlockSpec((tile, 512), lambda b: (b, 0)),
        compiler_params=pltpu.CompilerParams(
            dimension_semantics=("arbitrary",), vmem_limit_bytes=60 * 1024 * 1024
        ),
        name="last",
    )(cur, left_basis, last)


def solution(mesh):
    return jax.shard_map(
        per_device,
        mesh=mesh,
        in_specs=(
            P(("leaf", "rows"), None),
            P(("leaf", "rows"), None),
            P(("leaf", "rows"), None, None),
            P(None, ("leaf", "rows"), None),
            P(None, ("leaf", "rows"), None),
            P(),
            P(),
        ),
        out_specs=P(("leaf", "rows"), None),
        check_vma=False,
    )
```

```python
import jax
import jax.numpy as jnp
from jax import lax
from jax.experimental import pallas as pl
from jax.experimental.pallas import tpu as pltpu
from jax.sharding import PartitionSpec as P

F32 = jnp.float32
BF16 = jnp.bfloat16
MESH = pl.DeviceIdType.MESH
TN = (((0,), (0,)), ((), ()))
NT = (((1,), (1,)), ((), ()))
NN = (((1,), (0,)), ((), ()))
CHUNKS = 6
PER = 3
CHUNK = 256 * PER
GRAM_LANES = (slice(0, 384), slice(384, 640), slice(640, 768))


def mm(a, b, dims=NN):
    return lax.dot_general(a, b, dims, preferred_element_type=F32)


def halves(x):
    hi = x.astype(BF16)
    return hi, (x - hi.astype(F32)).astype(BF16)


def side_by_side(x):
    return jnp.concatenate(halves(x), axis=1)


def mm3(x, w_hi, w_lo):
    hi, lo = halves(x)
    return mm(hi, w_hi) + mm(lo, w_hi) + mm(hi, w_lo)


def one_hot(row, count):
    width = row.shape[1]
    spot = lax.broadcasted_iota(jnp.int32, (count, width), 0)
    return jnp.where(spot == jnp.broadcast_to(row, (count, width)), 1.0, 0.0).astype(BF16)


def rdma(src, dst, ssem, rsem, where):
    return pltpu.make_async_remote_copy(
        src_ref=src, dst_ref=dst, send_sem=ssem, recv_sem=rsem, device_id=where, device_id_type=MESH
    )


def main_kernel(
    rhs_hbm, order_ref, inv_hbm, right_hbm, left_hbm, perm_ref, joined_hbm, cur_hbm, last_ref,
    rhs, inv, right, left, cur, folded, turned, nodes, half_nodes, w_hi, w_lo, pairs, gram,
    coef, share0, shares, rest, mine0, gparts, gsum, ones, pair2, quad3,
    rhs_sem, inv_sem, right_sem, rest_sem, left_sem, node_sem, out_sem,
    s0, r0, sg, rg, sga, rga, ss, rs, sc, rc, se, re,
):
    leaf = lax.axis_index("leaf")
    row = lax.axis_index("rows")
    near = {"rows": lax.rem(row + 1, 16)}

    def rows_of(chunk):
        return pl.ds(pl.multiple_of(chunk * CHUNK, CHUNK), CHUNK)

    def load(chunk):
        spot = rows_of(chunk)
        blocks = pl.ds(chunk * PER, PER)
        return (
            pltpu.make_async_copy(rhs_hbm.at[spot], rhs.at[spot], rhs_sem.at[chunk]),
            pltpu.make_async_copy(inv_hbm.at[blocks], inv.at[blocks], inv_sem.at[chunk]),
            pltpu.make_async_copy(
                right_hbm.at[pl.ds(0, 2), spot], right.at[pl.ds(0, 2), spot], right_sem.at[chunk]
            ),
        )

    for chunk in range(2):
        for copy in load(chunk):
            copy.start()
    left_copy = pltpu.make_async_copy(left_hbm.at[pl.ds(0, 3)], left, left_sem)
    rest_copy = pltpu.make_async_copy(right_hbm.at[pl.ds(2, 2)], right.at[pl.ds(2, 2)], rest_sem)
    node_copies = [
        pltpu.make_async_copy(joined_hbm.at[leaf], nodes.at[0], node_sem.at[0]),
        pltpu.make_async_copy(joined_hbm.at[8 + leaf // 2], nodes.at[1], node_sem.at[1]),
    ]
    for level in range(2, 4):
        node = 16 - 16 // 2**level + leaf // 2**level
        side = leaf // 2 ** (level - 1) % 2
        node_copies.append(
            pltpu.make_async_copy(
                joined_hbm.at[node, pl.ds(side * 128, 128)], half_nodes.at[level - 2], node_sem.at[level]
            )
        )

    core = leaf % 2
    chip = leaf - core

    def each_row(body):
        for off in range(1, 16):
            body(lax.rem(row + off, 16))

    def each_owner(body):
        for off in range(1, 16):
            body(core, lax.rem(row + off, 16))
        for off in range(16):
            body(1 - core, lax.rem(row + off, 16))

    def place_of(side, q):
        return {"leaf": chip + side, "rows": q}

    barrier = pltpu.get_barrier_semaphore()
    each_owner(
        lambda side, q: pl.semaphore_signal(barrier, inc=1, device_id=place_of(side, q), device_id_type=MESH)
    )
    for off in range(1, 4):
        pl.semaphore_signal(
            barrier, inc=1, device_id={"leaf": lax.rem(leaf + 2 * off, 8)}, device_id_type=MESH
        )

    def solve_leaves(chunk):
        for i in range(PER):
            block = chunk * PER + i
            spot = slice(block * 256, block * 256 + 256)
            moved = mm(one_hot(order_ref[block : block + 1, :], 256), inv[block], NT).astype(BF16)
            inv[block] = moved
            basis = jnp.concatenate([right[0, spot, :], right[1, spot, :]], axis=1)
            hi, lo = halves(mm(moved, basis))
            part = slice(i * 256, i * 256 + 256)
            folded[chunk % 2, 0, part, :] = hi
            folded[chunk % 2, 1, part, :] = lo
        turned[chunk] = jnp.transpose(rhs[chunk * CHUNK : chunk * CHUNK + CHUNK, :])

    def project_first(chunk):
        cols = turned[chunk]
        terms = mm(cols, folded[chunk % 2, 0]) + mm(cols, folded[chunk % 2, 1])
        pairs[0] = terms if chunk == 0 else pairs[0] + terms

    for chunk in range(CHUNKS):
        for copy in load(chunk):
            copy.wait()
        if chunk + 2 < CHUNKS:
            for copy in load(chunk + 2):
                copy.start()
        else:
            for copy in ((left_copy,), (*node_copies, rest_copy))[chunk + 2 - CHUNKS]:
                copy.start()
        if chunk > 0:
            project_first(chunk - 1)
        solve_leaves(chunk)
    project_first(CHUNKS - 1)

    pl.semaphore_wait(barrier, 34)

    def send0(q):
        src = pairs.at[0, pl.ds(q * 32, 32), pl.ds(0, 128)]
        return rdma(src, share0.at[row], s0, r0, {"rows": q})

    each_row(lambda q: send0(q).start())
    share0[row] = pairs[0, pl.ds(row * 32, 32), 0:128]
    all0 = share0.at[pl.ds(0, 15)]

    left_copy.wait()
    rest_copy.wait()
    gram[...] = jnp.zeros_like(gram)
    pairs[1] = jnp.zeros_like(pairs[1])

    def multiply(chunk, carry):
        spot = rows_of(chunk)
        basis = [right[level, spot, :] for level in range(1, 4)]
        for low in range(3):
            gram[:, GRAM_LANES[low]] += mm(left[low, spot, :], jnp.concatenate(basis[low:], axis=1), TN)
        return carry

    lax.fori_loop(0, CHUNKS, multiply, 0)

    def send_gram(q):
        return rdma(gram.at[pl.ds(q * 8, 8), pl.ds(384, 384)], gparts.at[row], sg, rg, {"rows": q})

    each_row(lambda q: send_gram(q).start())
    gparts[row] = gram[pl.ds(row * 8, 8), 384:768]

    for copy in node_copies:
        copy.wait()
    start = 0
    for level in range(4):
        hot = one_hot(perm_ref[level : level + 1, :], 128)
        hi, lo = halves(nodes[level] if level < 2 else half_nodes[level - 2])
        count = hi.shape[0]
        for side in range(2):
            cut = slice(side * 128, side * 128 + 128)
            w_hi[cut, start : start + count] = mm(hot, hi[:, cut], NT).astype(BF16)
            w_lo[cut, start : start + count] = mm(hot, lo[:, cut], NT).astype(BF16)
        start += count

    rdma(all0, all0, s0, r0, near).wait_recv()
    low_child = share0[0]
    high_child = share0[8]
    for i in range(1, 8):
        low_child = low_child + share0[i]
        high_child = high_child + share0[8 + i]
    c0 = mm3(jnp.concatenate([low_child, high_child], axis=1), w_hi[:, 0:256], w_lo[:, 0:256])
    mine0[0] = c0[:, 0:128]
    mine0[1] = c0[:, 128:256]
    own = pl.ds(row * 32, 32)

    def send_c0(q):
        return rdma(mine0.at[q // 8], coef.at[0, own], sc.at[0], rc.at[0], {"rows": q})

    each_row(lambda q: send_c0(q).start())
    coef[0, own] = mine0[row // 8]

    def gathered(level):
        spot = coef.at[level, pl.ds(0, 480)]
        rdma(spot, spot, sc.at[level], rc.at[level], near).wait_recv()

    all_parts = gparts.at[pl.ds(0, 15)]
    rdma(all_parts, all_parts, sg, rg, near).wait_recv()
    total = gparts[0]
    for i in range(1, 16):
        total = total + gparts[i]
    own8 = pl.ds(core * 128 + row * 8, 8)
    gsum[own8, :] = total

    def send_sum(side, q):
        return rdma(gsum.at[own8], gsum.at[own8], sga, rga, place_of(side, q))

    each_owner(lambda side, q: send_sum(side, q).start())

    def project_rest(chunk, carry):
        parts = []
        for i in range(PER):
            spot = pl.ds(pl.multiple_of(chunk * CHUNK + i * 256, 256), 256)
            basis = jnp.concatenate([right[2, spot, :], right[3, spot, :]], axis=1)
            parts.append(halves(mm(inv[chunk * PER + i], basis)))
        cols = turned[chunk]
        hi = jnp.concatenate([part[0] for part in parts], axis=0)
        lo = jnp.concatenate([part[1] for part in parts], axis=0)
        pairs[1] += mm(cols, hi) + mm(cols, lo)
        return carry

    lax.fori_loop(0, CHUNKS, project_rest, 0)

    gathered(0)
    c0_hi, c0_lo = halves(coef[0])

    def send_rest(level, side, q):
        return rdma(
            rest.at[level - 1, pl.ds(q * 32 + side * 16, 16)], shares.at[level - 1, leaf % 2 * 16 + row],
            ss.at[level - 1], rs.at[level - 1], place_of(side, q),
        )

    own16 = pl.ds(row * 32 + core * 16, 16)
    for level in range(1, 4):
        lanes = slice(level * 128 - 128, level * 128)
        g_hi, g_lo = halves(gram[:, lanes])
        half = slice(level % 2 * 128, level % 2 * 128 + 128)
        taken = mm(c0_hi, g_hi) + mm(c0_lo, g_hi) + mm(c0_hi, g_lo)
        rest[level - 1] = pairs[level // 2, :, half] - taken
        each_owner(lambda side, q: send_rest(level, side, q).start())
        shares[level - 1, core * 16 + row] = rest[level - 1, own16]

    first = jnp.concatenate([c0_hi, c0_lo], axis=1)

    def correct_first(chunk, carry):
        for i in range(PER):
            spot = pl.ds(pl.multiple_of(chunk * CHUNK + i * 256, 256), 256)
            basis = left[0, spot, :]
            taken = mm(jnp.concatenate([basis, basis], axis=1), first, NT)
            cur[spot, :] = mm(inv[chunk * PER + i], rhs[spot, :], TN) - taken
        return carry

    lax.fori_loop(0, CHUNKS, correct_first, 0)

    def arrived(level):
        spot = shares.at[level - 1, pl.ds(0, 31)]
        rdma(spot, spot, ss.at[level - 1], rs.at[level - 1], near).wait_recv()

    def summed(level, start, count):
        value = shares[level - 1, start]
        for i in range(start + 1, start + count):
            value = value + shares[level - 1, i]
        return value

    def send_c(level, side, q):
        source = ones.at[side] if level == 1 else coef.at[level, own16]
        return rdma(source, coef.at[level, own16], sc.at[level], rc.at[level], place_of(side, q))

    def z_sends(level, buf):
        count = 2 ** (level - 1)
        base = leaf // (2 * count) * (2 * count) + core
        spot = leaf // 2 % count
        return [
            rdma(
                buf.at[spot], buf.at[spot], se.at[level - 2], re.at[level - 2],
                {"leaf": base + 2 * lax.rem(spot + off, count)},
            )
            for off in range(1, count)
        ]

    def begin(level, buf, value):
        buf[leaf // 2 % 2 ** (level - 1)] = value
        for copy in z_sends(level, buf):
            copy.start()

    def finish(level, buf):
        count = 2 ** (level - 1)
        spot = buf.at[pl.ds(0, count - 1)]
        rdma(spot, spot, se.at[level - 2], re.at[level - 2], near).wait_recv()
        half = count // 2
        low, high = buf[0], buf[half]
        for i in range(1, half):
            low = low + buf[i]
            high = high + buf[half + i]
        cut = slice(256 + level * 128, 384 + level * 128)
        c = mm3(jnp.concatenate([low, high], axis=1), w_hi[:, cut], w_lo[:, cut])
        coef[level, own16] = c
        return c

    sums = gsum.at[pl.ds(0, 248)]
    rdma(sums, sums, sga, rga, near).wait_recv()
    g1_hi, g1_lo = halves(gsum[:, 0:256])
    g2_hi, g2_lo = halves(gsum[:, 256:384])
    arrived(1)
    c1 = mm3(
        jnp.concatenate([summed(1, 0, 16), summed(1, 16, 16)], axis=1), w_hi[:, 256:512], w_lo[:, 256:512]
    )
    taken = mm3(c1, g1_hi, g1_lo)
    arrived(2)
    begin(2, pair2, summed(2, 0, 32) - taken[:, 0:128])
    ones[0] = c1[:, 0:128]
    ones[1] = c1[:, 128:256]
    each_owner(lambda side, q: send_c(1, side, q).start())
    coef[1, own16] = ones[core]
    arrived(3)
    part3 = summed(3, 0, 32) - taken[:, 128:256]
    c2 = finish(2, pair2)
    begin(3, quad3, part3 - mm3(jnp.concatenate([c2, c2], axis=1), g2_hi, g2_lo))
    each_owner(lambda side, q: send_c(2, side, q).start())
    finish(3, quad3)
    each_owner(lambda side, q: send_c(3, side, q).start())

    def spread(level):
        spot = coef.at[level, pl.ds(0, 496)]
        return rdma(spot, spot, sc.at[level], rc.at[level], near)

    spread(1).wait_recv()
    spread(2).wait_recv()
    middle = jnp.concatenate([side_by_side(coef[1]), side_by_side(coef[2])], axis=1)

    def store(chunk):
        spot = rows_of(chunk)
        return pltpu.make_async_copy(cur.at[spot], cur_hbm.at[spot], out_sem.at[chunk])

    def correct_middle(chunk, carry):
        spot = rows_of(chunk)
        one, two = left[1, spot, :], left[2, spot, :]
        cur[spot, :] = cur[spot, :] - mm(jnp.concatenate([one, one, two, two], axis=1), middle, NT)
        store(chunk).start()
        return carry

    lax.fori_loop(0, CHUNKS, correct_middle, 0)
    spread(3).wait_recv()
    last_ref[...] = side_by_side(coef[3])

    rdma(all0, all0, s0, r0, near).wait_send()
    rdma(all_parts, all_parts, sg, rg, near).wait_send()
    rdma(sums, sums, sga, rga, near).wait_send()
    span = coef.at[0, pl.ds(0, 480)]
    rdma(span, span, sc.at[0], rc.at[0], near).wait_send()
    for level in range(1, 4):
        spread(level).wait_send()
        span = shares.at[level - 1, pl.ds(0, 31)]
        rdma(span, span, ss.at[level - 1], rs.at[level - 1], near).wait_send()
    for level, buf in ((2, pair2), (3, quad3)):
        span = buf.at[pl.ds(0, 2 ** (level - 1) - 1)]
        rdma(span, span, se.at[level - 2], re.at[level - 2], near).wait_send()
    for chunk in range(CHUNKS):
        store(chunk).wait()


def last_kernel(cur_ref, left_ref, last_ref, out_ref):
    basis = left_ref[...]
    out_ref[...] = cur_ref[...] - mm(jnp.concatenate([basis, basis], axis=1), last_ref[...], NT)


def per_device(rhs, leaf_order, leaf_inv, right_basis, left_basis, rank_perm, joined):
    blocks = leaf_inv.shape[0]
    count = rhs.shape[0]
    dma = pltpu.SemaphoreType.DMA
    vmem = pl.BlockSpec(memory_space=pltpu.VMEM)
    hbm = pl.BlockSpec(memory_space=pl.ANY)
    cur, last = pl.pallas_call(
        main_kernel,
        out_shape=(jax.ShapeDtypeStruct(rhs.shape, F32), jax.ShapeDtypeStruct((512, 256), BF16)),
        in_specs=[hbm, vmem, hbm, hbm, hbm, vmem, hbm],
        out_specs=(hbm, vmem),
        scratch_shapes=[
            pltpu.VMEM((count, 512), BF16),
            pltpu.VMEM((blocks, 256, 256), BF16),
            pltpu.VMEM((4, count, 128), BF16),
            pltpu.VMEM((3, count, 128), BF16),
            pltpu.VMEM((count, 512), F32),
            pltpu.VMEM((2, 2, CHUNK, 256), BF16),
            pltpu.VMEM((CHUNKS, 512, CHUNK), BF16),
            pltpu.VMEM((2, 256, 256), F32),
            pltpu.VMEM((2, 128, 256), F32),
            pltpu.VMEM((256, 768), BF16),
            pltpu.VMEM((256, 768), BF16),
            pltpu.VMEM((2, 512, 256), F32),
            pltpu.VMEM((128, 768), F32),
            pltpu.VMEM((4, 512, 128), F32),
            pltpu.VMEM((16, 32, 128), F32),
            pltpu.VMEM((3, 32, 16, 128), F32),
            pltpu.VMEM((3, 512, 128), F32),
            pltpu.VMEM((2, 32, 128), F32),
            pltpu.VMEM((16, 8, 384), F32),
            pltpu.VMEM((256, 384), F32),
            pltpu.VMEM((2, 16, 128), F32),
            pltpu.VMEM((2, 16, 128), F32),
            pltpu.VMEM((4, 16, 128), F32),
            dma((CHUNKS,)), dma((CHUNKS,)), dma((CHUNKS,)), dma, dma, dma((4,)), dma((CHUNKS,)),
            dma, dma, dma, dma, dma, dma, dma((3,)), dma((3,)), dma((4,)), dma((4,)), dma((2,)), dma((2,)),
        ],
        compiler_params=pltpu.CompilerParams(
            collective_id=0, has_side_effects=True, vmem_limit_bytes=56 * 1024 * 1024
        ),
        name="main",
    )(rhs, leaf_order, leaf_inv, right_basis, left_basis, rank_perm, joined)

    tile = 768
    return pl.pallas_call(
        last_kernel,
        out_shape=jax.ShapeDtypeStruct(rhs.shape, F32),
        grid=(count // tile,),
        in_specs=[
            pl.BlockSpec((tile, 512), lambda b: (b, 0)),
            pl.BlockSpec((None, tile, 128), lambda b: (3, b, 0)),
            pl.BlockSpec((512, 256), lambda b: (0, 0)),
        ],
        out_specs=pl.BlockSpec((tile, 512), lambda b: (b, 0)),
        compiler_params=pltpu.CompilerParams(
            dimension_semantics=("arbitrary",), vmem_limit_bytes=60 * 1024 * 1024
        ),
        name="last",
    )(cur, left_basis, last)


def solution(mesh):
    return jax.shard_map(
        per_device,
        mesh=mesh,
        in_specs=(
            P(("leaf", "rows"), None),
            P(("leaf", "rows"), None),
            P(("leaf", "rows"), None, None),
            P(None, ("leaf", "rows"), None),
            P(None, ("leaf", "rows"), None),
            P(),
            P(),
        ),
        out_specs=P(("leaf", "rows"), None),
        check_vma=False,
    )
```

```python
import jax
import jax.numpy as jnp
from jax import lax
from jax.experimental import pallas as pl
from jax.experimental.pallas import tpu as pltpu
from jax.sharding import PartitionSpec as P

F32 = jnp.float32
BF16 = jnp.bfloat16
MESH = pl.DeviceIdType.MESH
TN = (((0,), (0,)), ((), ()))
NT = (((1,), (1,)), ((), ()))
NN = (((1,), (0,)), ((), ()))
CHUNKS = 6
PER = 3
CHUNK = 256 * PER
GRAM_LANES = (slice(0, 384), slice(384, 640), slice(640, 768))


def mm(a, b, dims=NN):
    return lax.dot_general(a, b, dims, preferred_element_type=F32)


def halves(x):
    hi = x.astype(BF16)
    return hi, (x - hi.astype(F32)).astype(BF16)


def side_by_side(x):
    return jnp.concatenate(halves(x), axis=1)


def mm3(x, w_hi, w_lo):
    hi, lo = halves(x)
    return mm(hi, w_hi) + mm(lo, w_hi) + mm(hi, w_lo)


def one_hot(row, count):
    width = row.shape[1]
    spot = lax.broadcasted_iota(jnp.int32, (count, width), 0)
    return jnp.where(spot == jnp.broadcast_to(row, (count, width)), 1.0, 0.0).astype(BF16)


def rdma(src, dst, ssem, rsem, where):
    return pltpu.make_async_remote_copy(
        src_ref=src, dst_ref=dst, send_sem=ssem, recv_sem=rsem, device_id=where, device_id_type=MESH
    )


def main_kernel(
    rhs_hbm, order_ref, inv_hbm, right_hbm, left_hbm, perm_ref, joined_hbm, cur_hbm, last_ref,
    rhs, inv, right, left, cur, folded, turned, nodes, half_nodes, w_hi, w_lo, pairs, gram,
    coef, share0, shares, rest, mine0, gparts, gsum, ones, pair2, quad3,
    rhs_sem, inv_sem, right_sem, rest_sem, left_sem, node_sem, out_sem,
    s0, r0, sg, rg, sga, rga, ss, rs, sc, rc, se, re,
):
    leaf = lax.axis_index("leaf")
    row = lax.axis_index("rows")
    near = {"rows": lax.rem(row + 1, 16)}

    def rows_of(chunk):
        return pl.ds(pl.multiple_of(chunk * CHUNK, CHUNK), CHUNK)

    def load(chunk):
        spot = rows_of(chunk)
        blocks = pl.ds(chunk * PER, PER)
        return (
            pltpu.make_async_copy(rhs_hbm.at[spot], rhs.at[spot], rhs_sem.at[chunk]),
            pltpu.make_async_copy(inv_hbm.at[blocks], inv.at[blocks], inv_sem.at[chunk]),
            pltpu.make_async_copy(
                right_hbm.at[pl.ds(0, 2), spot], right.at[pl.ds(0, 2), spot], right_sem.at[chunk]
            ),
        )

    for chunk in range(2):
        for copy in load(chunk):
            copy.start()
    left_copy = pltpu.make_async_copy(left_hbm.at[pl.ds(0, 3)], left, left_sem)
    rest_copy = pltpu.make_async_copy(right_hbm.at[pl.ds(2, 2)], right.at[pl.ds(2, 2)], rest_sem)
    node_copies = [
        pltpu.make_async_copy(joined_hbm.at[leaf], nodes.at[0], node_sem.at[0]),
        pltpu.make_async_copy(joined_hbm.at[8 + leaf // 2], nodes.at[1], node_sem.at[1]),
    ]
    for level in range(2, 4):
        node = 16 - 16 // 2**level + leaf // 2**level
        side = leaf // 2 ** (level - 1) % 2
        node_copies.append(
            pltpu.make_async_copy(
                joined_hbm.at[node, pl.ds(side * 128, 128)], half_nodes.at[level - 2], node_sem.at[level]
            )
        )

    core = leaf % 2
    chip = leaf - core

    def each_row(body):
        for off in range(1, 16):
            body(lax.rem(row + off, 16))

    def each_owner(body):
        for off in range(1, 16):
            body(core, lax.rem(row + off, 16))
        for off in range(16):
            body(1 - core, lax.rem(row + off, 16))

    def place_of(side, q):
        return {"leaf": chip + side, "rows": q}

    barrier = pltpu.get_barrier_semaphore()
    each_owner(
        lambda side, q: pl.semaphore_signal(barrier, inc=1, device_id=place_of(side, q), device_id_type=MESH)
    )
    for off in range(1, 4):
        pl.semaphore_signal(
            barrier, inc=1, device_id={"leaf": lax.rem(leaf + 2 * off, 8)}, device_id_type=MESH
        )

    def solve_leaves(chunk):
        for i in range(PER):
            block = chunk * PER + i
            spot = slice(block * 256, block * 256 + 256)
            moved = mm(one_hot(order_ref[block : block + 1, :], 256), inv[block], NT).astype(BF16)
            inv[block] = moved
            basis = jnp.concatenate([right[0, spot, :], right[1, spot, :]], axis=1)
            hi, lo = halves(mm(moved, basis))
            part = slice(i * 256, i * 256 + 256)
            folded[chunk % 2, 0, part, :] = hi
            folded[chunk % 2, 1, part, :] = lo
        turned[chunk] = jnp.transpose(rhs[chunk * CHUNK : chunk * CHUNK + CHUNK, :])

    def project_first(chunk):
        cols = turned[chunk]
        terms = mm(cols, folded[chunk % 2, 0]) + mm(cols, folded[chunk % 2, 1])
        pairs[0] = terms if chunk == 0 else pairs[0] + terms

    for chunk in range(CHUNKS):
        for copy in load(chunk):
            copy.wait()
        if chunk + 2 < CHUNKS:
            for copy in load(chunk + 2):
                copy.start()
        else:
            for copy in ((left_copy,), (*node_copies, rest_copy))[chunk + 2 - CHUNKS]:
                copy.start()
        if chunk > 0:
            project_first(chunk - 1)
        solve_leaves(chunk)
    project_first(CHUNKS - 1)

    pl.semaphore_wait(barrier, 34)

    def send0(q):
        src = pairs.at[0, pl.ds(q * 32, 32), pl.ds(0, 128)]
        return rdma(src, share0.at[row], s0, r0, {"rows": q})

    each_row(lambda q: send0(q).start())
    share0[row] = pairs[0, pl.ds(row * 32, 32), 0:128]
    all0 = share0.at[pl.ds(0, 15)]

    left_copy.wait()
    rest_copy.wait()
    gram[...] = jnp.zeros_like(gram)
    pairs[1] = jnp.zeros_like(pairs[1])

    def multiply(chunk, carry):
        spot = rows_of(chunk)
        basis = [right[level, spot, :] for level in range(1, 4)]
        for low in range(3):
            gram[:, GRAM_LANES[low]] += mm(left[low, spot, :], jnp.concatenate(basis[low:], axis=1), TN)
        return carry

    lax.fori_loop(0, CHUNKS, multiply, 0)

    def send_gram(q):
        return rdma(gram.at[pl.ds(q * 8, 8), pl.ds(384, 384)], gparts.at[row], sg, rg, {"rows": q})

    each_row(lambda q: send_gram(q).start())
    gparts[row] = gram[pl.ds(row * 8, 8), 384:768]

    for copy in node_copies:
        copy.wait()
    start = 0
    for level in range(4):
        hot = one_hot(perm_ref[level : level + 1, :], 128)
        hi, lo = halves(nodes[level] if level < 2 else half_nodes[level - 2])
        count = hi.shape[0]
        for side in range(2):
            cut = slice(side * 128, side * 128 + 128)
            w_hi[cut, start : start + count] = mm(hot, hi[:, cut], NT).astype(BF16)
            w_lo[cut, start : start + count] = mm(hot, lo[:, cut], NT).astype(BF16)
        start += count

    rdma(all0, all0, s0, r0, near).wait_recv()
    low_child = share0[0]
    high_child = share0[8]
    for i in range(1, 8):
        low_child = low_child + share0[i]
        high_child = high_child + share0[8 + i]
    c0 = mm3(jnp.concatenate([low_child, high_child], axis=1), w_hi[:, 0:256], w_lo[:, 0:256])
    mine0[0] = c0[:, 0:128]
    mine0[1] = c0[:, 128:256]
    own = pl.ds(row * 32, 32)

    def send_c0(q):
        return rdma(mine0.at[q // 8], coef.at[0, own], sc.at[0], rc.at[0], {"rows": q})

    each_row(lambda q: send_c0(q).start())
    coef[0, own] = mine0[row // 8]

    def gathered(level):
        spot = coef.at[level, pl.ds(0, 480)]
        rdma(spot, spot, sc.at[level], rc.at[level], near).wait_recv()

    all_parts = gparts.at[pl.ds(0, 15)]
    rdma(all_parts, all_parts, sg, rg, near).wait_recv()
    total = gparts[0]
    for i in range(1, 16):
        total = total + gparts[i]
    own8 = pl.ds(core * 128 + row * 8, 8)
    gsum[own8, :] = total

    def send_sum(side, q):
        return rdma(gsum.at[own8], gsum.at[own8], sga, rga, place_of(side, q))

    each_owner(lambda side, q: send_sum(side, q).start())

    def project_rest(chunk, carry):
        parts = []
        for i in range(PER):
            spot = pl.ds(pl.multiple_of(chunk * CHUNK + i * 256, 256), 256)
            basis = jnp.concatenate([right[2, spot, :], right[3, spot, :]], axis=1)
            parts.append(halves(mm(inv[chunk * PER + i], basis)))
        cols = turned[chunk]
        hi = jnp.concatenate([part[0] for part in parts], axis=0)
        lo = jnp.concatenate([part[1] for part in parts], axis=0)
        pairs[1] += mm(cols, hi) + mm(cols, lo)
        return carry

    lax.fori_loop(0, 4, project_rest, 0)

    gathered(0)
    c0_hi, c0_lo = halves(coef[0])

    def send_rest(level, side, q):
        return rdma(
            rest.at[level - 1, pl.ds(q * 32 + side * 16, 16)], shares.at[level - 1, leaf % 2 * 16 + row],
            ss.at[level - 1], rs.at[level - 1], place_of(side, q),
        )

    own16 = pl.ds(row * 32 + core * 16, 16)
    def update(level):
        lanes = slice(level * 128 - 128, level * 128)
        g_hi, g_lo = halves(gram[:, lanes])
        half = slice(level % 2 * 128, level % 2 * 128 + 128)
        taken = mm(c0_hi, g_hi) + mm(c0_lo, g_hi) + mm(c0_hi, g_lo)
        rest[level - 1] = pairs[level // 2, :, half] - taken
        each_owner(lambda side, q: send_rest(level, side, q).start())
        shares[level - 1, core * 16 + row] = rest[level - 1, own16]

    update(1)
    lax.fori_loop(4, CHUNKS, project_rest, 0)
    update(2)
    update(3)

    first = jnp.concatenate([c0_hi, c0_lo], axis=1)

    def correct_first(chunk, carry):
        for i in range(PER):
            spot = pl.ds(pl.multiple_of(chunk * CHUNK + i * 256, 256), 256)
            basis = left[0, spot, :]
            taken = mm(jnp.concatenate([basis, basis], axis=1), first, NT)
            cur[spot, :] = mm(inv[chunk * PER + i], rhs[spot, :], TN) - taken
        return carry

    lax.fori_loop(0, 2, correct_first, 0)

    def arrived(level):
        spot = shares.at[level - 1, pl.ds(0, 31)]
        rdma(spot, spot, ss.at[level - 1], rs.at[level - 1], near).wait_recv()

    def summed(level, start, count):
        value = shares[level - 1, start]
        for i in range(start + 1, start + count):
            value = value + shares[level - 1, i]
        return value

    def send_c(level, side, q):
        source = ones.at[side] if level == 1 else coef.at[level, own16]
        return rdma(source, coef.at[level, own16], sc.at[level], rc.at[level], place_of(side, q))

    def z_sends(level, buf):
        count = 2 ** (level - 1)
        base = leaf // (2 * count) * (2 * count) + core
        spot = leaf // 2 % count
        return [
            rdma(
                buf.at[spot], buf.at[spot], se.at[level - 2], re.at[level - 2],
                {"leaf": base + 2 * lax.rem(spot + off, count)},
            )
            for off in range(1, count)
        ]

    def begin(level, buf, value):
        buf[leaf // 2 % 2 ** (level - 1)] = value
        for copy in z_sends(level, buf):
            copy.start()

    def finish(level, buf):
        count = 2 ** (level - 1)
        spot = buf.at[pl.ds(0, count - 1)]
        rdma(spot, spot, se.at[level - 2], re.at[level - 2], near).wait_recv()
        half = count // 2
        low, high = buf[0], buf[half]
        for i in range(1, half):
            low = low + buf[i]
            high = high + buf[half + i]
        cut = slice(256 + level * 128, 384 + level * 128)
        c = mm3(jnp.concatenate([low, high], axis=1), w_hi[:, cut], w_lo[:, cut])
        coef[level, own16] = c
        return c

    sums = gsum.at[pl.ds(0, 248)]
    rdma(sums, sums, sga, rga, near).wait_recv()
    g1_hi, g1_lo = halves(gsum[:, 0:256])
    g2_hi, g2_lo = halves(gsum[:, 256:384])
    arrived(1)
    c1 = mm3(
        jnp.concatenate([summed(1, 0, 16), summed(1, 16, 16)], axis=1), w_hi[:, 256:512], w_lo[:, 256:512]
    )
    taken = mm3(c1, g1_hi, g1_lo)
    arrived(2)
    begin(2, pair2, summed(2, 0, 32) - taken[:, 0:128])
    ones[0] = c1[:, 0:128]
    ones[1] = c1[:, 128:256]
    each_owner(lambda side, q: send_c(1, side, q).start())
    coef[1, own16] = ones[core]
    lax.fori_loop(2, 4, correct_first, 0)
    arrived(3)
    part3 = summed(3, 0, 32) - taken[:, 128:256]
    c2 = finish(2, pair2)
    begin(3, quad3, part3 - mm3(jnp.concatenate([c2, c2], axis=1), g2_hi, g2_lo))
    each_owner(lambda side, q: send_c(2, side, q).start())
    lax.fori_loop(4, CHUNKS, correct_first, 0)
    finish(3, quad3)
    each_owner(lambda side, q: send_c(3, side, q).start())

    def spread(level):
        spot = coef.at[level, pl.ds(0, 496)]
        return rdma(spot, spot, sc.at[level], rc.at[level], near)

    spread(1).wait_recv()
    spread(2).wait_recv()
    middle = jnp.concatenate([side_by_side(coef[1]), side_by_side(coef[2])], axis=1)

    def store(chunk):
        spot = rows_of(chunk)
        return pltpu.make_async_copy(cur.at[spot], cur_hbm.at[spot], out_sem.at[chunk])

    def correct_middle(chunk, carry):
        spot = rows_of(chunk)
        one, two = left[1, spot, :], left[2, spot, :]
        cur[spot, :] = cur[spot, :] - mm(jnp.concatenate([one, one, two, two], axis=1), middle, NT)
        store(chunk).start()
        return carry

    lax.fori_loop(0, CHUNKS, correct_middle, 0)
    spread(3).wait_recv()
    last_ref[...] = side_by_side(coef[3])

    rdma(all0, all0, s0, r0, near).wait_send()
    rdma(all_parts, all_parts, sg, rg, near).wait_send()
    rdma(sums, sums, sga, rga, near).wait_send()
    span = coef.at[0, pl.ds(0, 480)]
    rdma(span, span, sc.at[0], rc.at[0], near).wait_send()
    for level in range(1, 4):
        spread(level).wait_send()
        span = shares.at[level - 1, pl.ds(0, 31)]
        rdma(span, span, ss.at[level - 1], rs.at[level - 1], near).wait_send()
    for level, buf in ((2, pair2), (3, quad3)):
        span = buf.at[pl.ds(0, 2 ** (level - 1) - 1)]
        rdma(span, span, se.at[level - 2], re.at[level - 2], near).wait_send()
    for chunk in range(CHUNKS):
        store(chunk).wait()


def last_kernel(cur_ref, left_ref, last_ref, out_ref):
    basis = left_ref[...]
    out_ref[...] = cur_ref[...] - mm(jnp.concatenate([basis, basis], axis=1), last_ref[...], NT)


def per_device(rhs, leaf_order, leaf_inv, right_basis, left_basis, rank_perm, joined):
    blocks = leaf_inv.shape[0]
    count = rhs.shape[0]
    dma = pltpu.SemaphoreType.DMA
    vmem = pl.BlockSpec(memory_space=pltpu.VMEM)
    hbm = pl.BlockSpec(memory_space=pl.ANY)
    cur, last = pl.pallas_call(
        main_kernel,
        out_shape=(jax.ShapeDtypeStruct(rhs.shape, F32), jax.ShapeDtypeStruct((512, 256), BF16)),
        in_specs=[hbm, vmem, hbm, hbm, hbm, vmem, hbm],
        out_specs=(hbm, vmem),
        scratch_shapes=[
            pltpu.VMEM((count, 512), BF16),
            pltpu.VMEM((blocks, 256, 256), BF16),
            pltpu.VMEM((4, count, 128), BF16),
            pltpu.VMEM((3, count, 128), BF16),
            pltpu.VMEM((count, 512), F32),
            pltpu.VMEM((2, 2, CHUNK, 256), BF16),
            pltpu.VMEM((CHUNKS, 512, CHUNK), BF16),
            pltpu.VMEM((2, 256, 256), F32),
            pltpu.VMEM((2, 128, 256), F32),
            pltpu.VMEM((256, 768), BF16),
            pltpu.VMEM((256, 768), BF16),
            pltpu.VMEM((2, 512, 256), F32),
            pltpu.VMEM((128, 768), F32),
            pltpu.VMEM((4, 512, 128), F32),
            pltpu.VMEM((16, 32, 128), F32),
            pltpu.VMEM((3, 32, 16, 128), F32),
            pltpu.VMEM((3, 512, 128), F32),
            pltpu.VMEM((2, 32, 128), F32),
            pltpu.VMEM((16, 8, 384), F32),
            pltpu.VMEM((256, 384), F32),
            pltpu.VMEM((2, 16, 128), F32),
            pltpu.VMEM((2, 16, 128), F32),
            pltpu.VMEM((4, 16, 128), F32),
            dma((CHUNKS,)), dma((CHUNKS,)), dma((CHUNKS,)), dma, dma, dma((4,)), dma((CHUNKS,)),
            dma, dma, dma, dma, dma, dma, dma((3,)), dma((3,)), dma((4,)), dma((4,)), dma((2,)), dma((2,)),
        ],
        compiler_params=pltpu.CompilerParams(
            collective_id=0, has_side_effects=True, vmem_limit_bytes=56 * 1024 * 1024
        ),
        name="main",
    )(rhs, leaf_order, leaf_inv, right_basis, left_basis, rank_perm, joined)

    tile = 768
    return pl.pallas_call(
        last_kernel,
        out_shape=jax.ShapeDtypeStruct(rhs.shape, F32),
        grid=(count // tile,),
        in_specs=[
            pl.BlockSpec((tile, 512), lambda b: (b, 0)),
            pl.BlockSpec((None, tile, 128), lambda b: (3, b, 0)),
            pl.BlockSpec((512, 256), lambda b: (0, 0)),
        ],
        out_specs=pl.BlockSpec((tile, 512), lambda b: (b, 0)),
        compiler_params=pltpu.CompilerParams(
            dimension_semantics=("arbitrary",), vmem_limit_bytes=60 * 1024 * 1024
        ),
        name="last",
    )(cur, left_basis, last)


def solution(mesh):
    return jax.shard_map(
        per_device,
        mesh=mesh,
        in_specs=(
            P(("leaf", "rows"), None),
            P(("leaf", "rows"), None),
            P(("leaf", "rows"), None, None),
            P(None, ("leaf", "rows"), None),
            P(None, ("leaf", "rows"), None),
            P(),
            P(),
        ),
        out_specs=P(("leaf", "rows"), None),
        check_vma=False,
    )
```

```python
import jax
import jax.numpy as jnp
from jax import lax
from jax.experimental import pallas as pl
from jax.experimental.pallas import tpu as pltpu
from jax.sharding import PartitionSpec as P

F32 = jnp.float32
BF16 = jnp.bfloat16
MESH = pl.DeviceIdType.MESH
TN = (((0,), (0,)), ((), ()))
NT = (((1,), (1,)), ((), ()))
NN = (((1,), (0,)), ((), ()))
CHUNKS = 6
PER = 3
CHUNK = 256 * PER
LAST_SPLIT = 4


def mm(a, b, dims=NN):
    return lax.dot_general(a, b, dims, preferred_element_type=F32)


def halves(x):
    hi = x.astype(BF16)
    return hi, (x - hi.astype(F32)).astype(BF16)


def side_by_side(x):
    return jnp.concatenate(halves(x), axis=1)


def mm3(x, w_hi, w_lo):
    hi, lo = halves(x)
    return mm(hi, w_hi) + mm(lo, w_hi) + mm(hi, w_lo)


def one_hot(row, count):
    width = row.shape[1]
    spot = lax.broadcasted_iota(jnp.int32, (count, width), 0)
    return jnp.where(spot == jnp.broadcast_to(row, (count, width)), 1.0, 0.0).astype(BF16)


def rdma(src, dst, ssem, rsem, where):
    return pltpu.make_async_remote_copy(
        src_ref=src, dst_ref=dst, send_sem=ssem, recv_sem=rsem, device_id=where, device_id_type=MESH
    )


def main_kernel(
    rhs_hbm, order_ref, inv_hbm, right_hbm, left_hbm, perm_ref, joined_hbm, cur_hbm, last_ref,
    rhs, inv, right, left, cur, folded, turned, nodes, half_nodes, w_hi, w_lo, pairs, gram, upper,
    coef, share0, shares, rest, mine0, gparts, gsum, ones, pair2, quad3,
    rhs_sem, inv_sem, right_sem, rest_sem, left_sem, node_sem, out_sem,
    s0, r0, sg, rg, sga, rga, ss, rs, sc, rc, se, re,
):
    leaf = lax.axis_index("leaf")
    row = lax.axis_index("rows")
    near = {"rows": lax.rem(row + 1, 16)}

    def rows_of(chunk):
        return pl.ds(pl.multiple_of(chunk * CHUNK, CHUNK), CHUNK)

    def load(chunk):
        spot = rows_of(chunk)
        blocks = pl.ds(chunk * PER, PER)
        return (
            pltpu.make_async_copy(rhs_hbm.at[spot], rhs.at[spot], rhs_sem.at[chunk]),
            pltpu.make_async_copy(inv_hbm.at[blocks], inv.at[blocks], inv_sem.at[chunk]),
            pltpu.make_async_copy(
                right_hbm.at[pl.ds(0, 2), spot], right.at[pl.ds(0, 2), spot], right_sem.at[chunk]
            ),
        )

    for chunk in range(2):
        for copy in load(chunk):
            copy.start()
    left_copy = pltpu.make_async_copy(left_hbm.at[pl.ds(0, 3)], left, left_sem)
    rest_copy = pltpu.make_async_copy(right_hbm.at[pl.ds(2, 2)], right.at[pl.ds(2, 2)], rest_sem)
    node_copies = [
        pltpu.make_async_copy(joined_hbm.at[leaf], nodes.at[0], node_sem.at[0]),
        pltpu.make_async_copy(joined_hbm.at[8 + leaf // 2], nodes.at[1], node_sem.at[1]),
    ]
    for level in range(2, 4):
        node = 16 - 16 // 2**level + leaf // 2**level
        side = leaf // 2 ** (level - 1) % 2
        node_copies.append(
            pltpu.make_async_copy(
                joined_hbm.at[node, pl.ds(side * 128, 128)], half_nodes.at[level - 2], node_sem.at[level]
            )
        )

    core = leaf % 2
    chip = leaf - core

    def each_row(body):
        for off in range(1, 16):
            body(lax.rem(row + off, 16))

    def each_owner(body):
        for off in range(1, 16):
            body(core, lax.rem(row + off, 16))
        for off in range(16):
            body(1 - core, lax.rem(row + off, 16))

    def place_of(side, q):
        return {"leaf": chip + side, "rows": q}

    barrier = pltpu.get_barrier_semaphore()
    each_owner(
        lambda side, q: pl.semaphore_signal(barrier, inc=1, device_id=place_of(side, q), device_id_type=MESH)
    )
    for off in range(1, 4):
        pl.semaphore_signal(
            barrier, inc=1, device_id={"leaf": lax.rem(leaf + 2 * off, 8)}, device_id_type=MESH
        )

    def solve_leaves(chunk):
        for i in range(PER):
            block = chunk * PER + i
            spot = slice(block * 256, block * 256 + 256)
            moved = mm(one_hot(order_ref[block : block + 1, :], 256), inv[block], NT).astype(BF16)
            inv[block] = moved
            basis = jnp.concatenate([right[0, spot, :], right[1, spot, :]], axis=1)
            hi, lo = halves(mm(moved, basis))
            part = slice(i * 256, i * 256 + 256)
            folded[chunk % 2, 0, part, :] = hi
            folded[chunk % 2, 1, part, :] = lo
        turned[chunk] = jnp.transpose(rhs[chunk * CHUNK : chunk * CHUNK + CHUNK, :])

    def project_first(chunk):
        cols = turned[chunk]
        terms = mm(jnp.concatenate([cols, cols], axis=1), folded[chunk % 2].reshape(2 * CHUNK, 256))
        pairs[0] = terms if chunk == 0 else pairs[0] + terms

    for chunk in range(CHUNKS):
        for copy in load(chunk):
            copy.wait()
        if chunk + 2 < CHUNKS:
            for copy in load(chunk + 2):
                copy.start()
        else:
            for copy in ((left_copy,), (*node_copies, rest_copy))[chunk + 2 - CHUNKS]:
                copy.start()
        if chunk > 0:
            project_first(chunk - 1)
        solve_leaves(chunk)
    project_first(CHUNKS - 1)

    pl.semaphore_wait(barrier, 34)

    def send0(q):
        src = pairs.at[0, pl.ds(q * 32, 32), pl.ds(0, 128)]
        return rdma(src, share0.at[row], s0, r0, {"rows": q})

    each_row(lambda q: send0(q).start())
    share0[row] = pairs[0, pl.ds(row * 32, 32), 0:128]
    all0 = share0.at[pl.ds(0, 15)]

    left_copy.wait()
    rest_copy.wait()
    gram[...] = jnp.zeros_like(gram)
    pairs[1] = jnp.zeros_like(pairs[1])

    def multiply(step, carry):
        spot = pl.ds(pl.multiple_of(step * 2 * CHUNK, 2 * CHUNK), 2 * CHUNK)

        def both(ref, one, two):
            return jnp.concatenate([ref[one, spot, :], ref[two, spot, :]], axis=1)

        gram[0] += mm(both(left, 0, 1), both(right, 2, 3), TN)
        gram[1] += mm(both(left, 0, 2), both(right, 1, 3), TN)
        return carry

    lax.fori_loop(0, CHUNKS // 2, multiply, 0)
    upper[:, 0:256] = gram[0, 128:256, :]
    upper[:, 256:384] = gram[1, 128:256, 128:256]

    def send_gram(q):
        return rdma(upper.at[pl.ds(q * 8, 8)], gparts.at[row], sg, rg, {"rows": q})

    each_row(lambda q: send_gram(q).start())
    gparts[row] = upper[pl.ds(row * 8, 8), :]

    for copy in node_copies:
        copy.wait()
    start = 0
    for level in range(4):
        hot = one_hot(perm_ref[level : level + 1, :], 128)
        hi, lo = halves(nodes[level] if level < 2 else half_nodes[level - 2])
        count = hi.shape[0]
        for side in range(2):
            cut = slice(side * 128, side * 128 + 128)
            w_hi[cut, start : start + count] = mm(hot, hi[:, cut], NT).astype(BF16)
            w_lo[cut, start : start + count] = mm(hot, lo[:, cut], NT).astype(BF16)
        start += count

    rdma(all0, all0, s0, r0, near).wait_recv()
    low_child = share0[0]
    high_child = share0[8]
    for i in range(1, 8):
        low_child = low_child + share0[i]
        high_child = high_child + share0[8 + i]
    c0 = mm3(jnp.concatenate([low_child, high_child], axis=1), w_hi[:, 0:256], w_lo[:, 0:256])
    mine0[0] = c0[:, 0:128]
    mine0[1] = c0[:, 128:256]
    own = pl.ds(row * 32, 32)

    def send_c0(q):
        return rdma(mine0.at[q // 8], coef.at[0, own], sc.at[0], rc.at[0], {"rows": q})

    each_row(lambda q: send_c0(q).start())
    coef[0, own] = mine0[row // 8]

    def gathered(level):
        spot = coef.at[level, pl.ds(0, 480)]
        rdma(spot, spot, sc.at[level], rc.at[level], near).wait_recv()

    all_parts = gparts.at[pl.ds(0, 15)]
    rdma(all_parts, all_parts, sg, rg, near).wait_recv()
    total = gparts[0]
    for i in range(1, 16):
        total = total + gparts[i]
    own8 = pl.ds(core * 128 + row * 8, 8)
    gsum[own8, :] = total

    def send_sum(side, q):
        return rdma(gsum.at[own8], gsum.at[own8], sga, rga, place_of(side, q))

    each_owner(lambda side, q: send_sum(side, q).start())

    def project_rest(start, count):
        total = pairs[1]
        for j in range(count):
            chunk = start + j
            parts = []
            for i in range(PER):
                spot = pl.ds(pl.multiple_of(chunk * CHUNK + i * 256, 256), 256)
                basis = jnp.concatenate([right[2, spot, :], right[3, spot, :]], axis=1)
                parts.append(halves(mm(inv[chunk * PER + i], basis)))
            cols = turned[chunk]
            hi = jnp.concatenate([part[0] for part in parts], axis=0)
            lo = jnp.concatenate([part[1] for part in parts], axis=0)
            total = total + mm(jnp.concatenate([cols, cols], axis=1), jnp.concatenate([hi, lo], axis=0))
        pairs[1] = total

    @pl.loop(0, 2)
    def _(step):
        project_rest(step * 2, 2)

    gathered(0)
    c0_hi, c0_lo = halves(coef[0])

    def send_rest(level, side, q):
        return rdma(
            rest.at[level - 1, pl.ds(q * 32 + side * 16, 16)], shares.at[level - 1, leaf % 2 * 16 + row],
            ss.at[level - 1], rs.at[level - 1], place_of(side, q),
        )

    own16 = pl.ds(row * 32 + core * 16, 16)
    def update(level):
        lanes = slice(128, 256) if level == 3 else slice(0, 128)
        g_hi, g_lo = halves(gram[1 if level == 1 else 0, 0:128, lanes])
        half = slice(level % 2 * 128, level % 2 * 128 + 128)
        taken = mm(c0_hi, g_hi) + mm(c0_lo, g_hi) + mm(c0_hi, g_lo)
        rest[level - 1] = pairs[level // 2, :, half] - taken
        each_owner(lambda side, q: send_rest(level, side, q).start())
        shares[level - 1, core * 16 + row] = rest[level - 1, own16]

    update(1)

    @pl.loop(4, CHUNKS)
    def _(chunk):
        project_rest(chunk, 1)

    update(2)
    update(3)

    first = jnp.concatenate([c0_hi, c0_lo], axis=1)

    def correct_first(chunk, carry):
        for i in range(PER):
            spot = pl.ds(pl.multiple_of(chunk * CHUNK + i * 256, 256), 256)
            basis = left[0, spot, :]
            taken = mm(jnp.concatenate([basis, basis], axis=1), first, NT)
            cur[spot, :] = mm(inv[chunk * PER + i], rhs[spot, :], TN) - taken
        return carry

    lax.fori_loop(0, 2, correct_first, 0)

    def arrived(level):
        spot = shares.at[level - 1, pl.ds(0, 31)]
        rdma(spot, spot, ss.at[level - 1], rs.at[level - 1], near).wait_recv()

    def summed(level, start, count):
        value = shares[level - 1, start]
        for i in range(start + 1, start + count):
            value = value + shares[level - 1, i]
        return value

    def send_c(level, side, q):
        source = ones.at[side] if level == 1 else coef.at[level, own16]
        return rdma(source, coef.at[level, own16], sc.at[level], rc.at[level], place_of(side, q))

    def z_sends(level, buf):
        count = 2 ** (level - 1)
        base = leaf // (2 * count) * (2 * count) + core
        spot = leaf // 2 % count
        return [
            rdma(
                buf.at[spot], buf.at[spot], se.at[level - 2], re.at[level - 2],
                {"leaf": base + 2 * lax.rem(spot + off, count)},
            )
            for off in range(1, count)
        ]

    def begin(level, buf, value):
        buf[leaf // 2 % 2 ** (level - 1)] = value
        for copy in z_sends(level, buf):
            copy.start()

    def finish(level, buf):
        count = 2 ** (level - 1)
        spot = buf.at[pl.ds(0, count - 1)]
        rdma(spot, spot, se.at[level - 2], re.at[level - 2], near).wait_recv()
        half = count // 2
        low, high = buf[0], buf[half]
        for i in range(1, half):
            low = low + buf[i]
            high = high + buf[half + i]
        cut = slice(256 + level * 128, 384 + level * 128)
        c = mm3(jnp.concatenate([low, high], axis=1), w_hi[:, cut], w_lo[:, cut])
        coef[level, own16] = c
        return c

    sums = gsum.at[pl.ds(0, 248)]
    rdma(sums, sums, sga, rga, near).wait_recv()
    g1_hi, g1_lo = halves(gsum[:, 0:256])
    g2_hi, g2_lo = halves(gsum[:, 256:384])
    arrived(1)
    c1 = mm3(
        jnp.concatenate([summed(1, 0, 16), summed(1, 16, 16)], axis=1), w_hi[:, 256:512], w_lo[:, 256:512]
    )
    taken = mm3(c1, g1_hi, g1_lo)
    arrived(2)
    begin(2, pair2, summed(2, 0, 32) - taken[:, 0:128])
    ones[0] = c1[:, 0:128]
    ones[1] = c1[:, 128:256]
    each_owner(lambda side, q: send_c(1, side, q).start())
    coef[1, own16] = ones[core]
    lax.fori_loop(2, 4, correct_first, 0)
    arrived(3)
    part3 = summed(3, 0, 32) - taken[:, 128:256]
    c2 = finish(2, pair2)
    begin(3, quad3, part3 - mm3(jnp.concatenate([c2, c2], axis=1), g2_hi, g2_lo))
    each_owner(lambda side, q: send_c(2, side, q).start())
    lax.fori_loop(4, CHUNKS, correct_first, 0)
    finish(3, quad3)
    each_owner(lambda side, q: send_c(3, side, q).start())

    def spread(level):
        spot = coef.at[level, pl.ds(0, 496)]
        return rdma(spot, spot, sc.at[level], rc.at[level], near)

    spread(1).wait_recv()
    spread(2).wait_recv()
    middle = jnp.concatenate([side_by_side(coef[1]), side_by_side(coef[2])], axis=1)

    def store(chunk):
        spot = rows_of(chunk)
        return pltpu.make_async_copy(cur.at[spot], cur_hbm.at[spot], out_sem.at[chunk])

    def correct_middle(chunk, carry):
        spot = rows_of(chunk)
        one, two = left[1, spot, :], left[2, spot, :]
        cur[spot, :] = cur[spot, :] - mm(jnp.concatenate([one, one, two, two], axis=1), middle, NT)
        store(chunk).start()
        return carry

    lax.fori_loop(0, CHUNKS, correct_middle, 0)
    spread(3).wait_recv()
    last_ref[...] = side_by_side(coef[3])

    rdma(all0, all0, s0, r0, near).wait_send()
    rdma(all_parts, all_parts, sg, rg, near).wait_send()
    rdma(sums, sums, sga, rga, near).wait_send()
    span = coef.at[0, pl.ds(0, 480)]
    rdma(span, span, sc.at[0], rc.at[0], near).wait_send()
    for level in range(1, 4):
        spread(level).wait_send()
        span = shares.at[level - 1, pl.ds(0, 31)]
        rdma(span, span, ss.at[level - 1], rs.at[level - 1], near).wait_send()
    for level, buf in ((2, pair2), (3, quad3)):
        span = buf.at[pl.ds(0, 2 ** (level - 1) - 1)]
        rdma(span, span, se.at[level - 2], re.at[level - 2], near).wait_send()
    for chunk in range(CHUNKS):
        store(chunk).wait()


def last_kernel(cur_hbm, left_hbm, last_hbm, out_hbm, cur, left, last, cur_sem, left_sem, last_sem, out_sem):
    part = CHUNK // LAST_SPLIT

    def parts(chunk):
        return [pl.ds(chunk * CHUNK + j * part, part) for j in range(LAST_SPLIT)]

    def reads(chunk):
        rows = pl.ds(chunk * CHUNK, CHUNK)
        copies = [pltpu.make_async_copy(left_hbm.at[3, rows], left.at[rows], left_sem.at[chunk])]
        for j, spot in enumerate(parts(chunk)):
            copies.append(pltpu.make_async_copy(cur_hbm.at[spot], cur.at[spot], cur_sem.at[chunk, j]))
        return copies

    def writes(chunk):
        return [
            pltpu.make_async_copy(cur.at[spot], out_hbm.at[spot], out_sem.at[chunk, j])
            for j, spot in enumerate(parts(chunk))
        ]

    last_copy = pltpu.make_async_copy(last_hbm, last, last_sem)
    last_copy.start()
    for chunk in range(CHUNKS):
        for copy in reads(chunk):
            copy.start()
    last_copy.wait()
    weights = last[...]
    for chunk in range(CHUNKS):
        for copy in reads(chunk):
            copy.wait()
        rows = slice(chunk * CHUNK, chunk * CHUNK + CHUNK)
        basis = left[rows, :]
        cur[rows, :] = cur[rows, :] - mm(jnp.concatenate([basis, basis], axis=1), weights, NT)
        for copy in writes(chunk):
            copy.start()
    for chunk in range(CHUNKS):
        for copy in writes(chunk):
            copy.wait()


def per_device(rhs, leaf_order, leaf_inv, right_basis, left_basis, rank_perm, joined):
    blocks = leaf_inv.shape[0]
    count = rhs.shape[0]
    dma = pltpu.SemaphoreType.DMA
    vmem = pl.BlockSpec(memory_space=pltpu.VMEM)
    hbm = pl.BlockSpec(memory_space=pl.ANY)
    cur, last = pl.pallas_call(
        main_kernel,
        out_shape=(jax.ShapeDtypeStruct(rhs.shape, F32), jax.ShapeDtypeStruct((512, 256), BF16)),
        in_specs=[hbm, vmem, hbm, hbm, hbm, vmem, hbm],
        out_specs=(hbm, vmem),
        scratch_shapes=[
            pltpu.VMEM((count, 512), BF16),
            pltpu.VMEM((blocks, 256, 256), BF16),
            pltpu.VMEM((4, count, 128), BF16),
            pltpu.VMEM((3, count, 128), BF16),
            pltpu.VMEM((count, 512), F32),
            pltpu.VMEM((2, 2, CHUNK, 256), BF16),
            pltpu.VMEM((CHUNKS, 512, CHUNK), BF16),
            pltpu.VMEM((2, 256, 256), F32),
            pltpu.VMEM((2, 128, 256), F32),
            pltpu.VMEM((256, 768), BF16),
            pltpu.VMEM((256, 768), BF16),
            pltpu.VMEM((2, 512, 256), F32),
            pltpu.VMEM((2, 256, 256), F32),
            pltpu.VMEM((128, 384), F32),
            pltpu.VMEM((4, 512, 128), F32),
            pltpu.VMEM((16, 32, 128), F32),
            pltpu.VMEM((3, 32, 16, 128), F32),
            pltpu.VMEM((3, 512, 128), F32),
            pltpu.VMEM((2, 32, 128), F32),
            pltpu.VMEM((16, 8, 384), F32),
            pltpu.VMEM((256, 384), F32),
            pltpu.VMEM((2, 16, 128), F32),
            pltpu.VMEM((2, 16, 128), F32),
            pltpu.VMEM((4, 16, 128), F32),
            dma((CHUNKS,)), dma((CHUNKS,)), dma((CHUNKS,)), dma, dma, dma((4,)), dma((CHUNKS,)),
            dma, dma, dma, dma, dma, dma, dma((3,)), dma((3,)), dma((4,)), dma((4,)), dma((2,)), dma((2,)),
        ],
        compiler_params=pltpu.CompilerParams(
            collective_id=0, has_side_effects=True, vmem_limit_bytes=56 * 1024 * 1024
        ),
        name="main",
    )(rhs, leaf_order, leaf_inv, right_basis, left_basis, rank_perm, joined)

    return pl.pallas_call(
        last_kernel,
        out_shape=jax.ShapeDtypeStruct(rhs.shape, F32),
        in_specs=[hbm, hbm, hbm],
        out_specs=hbm,
        scratch_shapes=[
            pltpu.VMEM((count, 512), F32),
            pltpu.VMEM((count, 128), BF16),
            pltpu.VMEM((512, 256), BF16),
            dma((CHUNKS, LAST_SPLIT)), dma((CHUNKS,)), dma, dma((CHUNKS, LAST_SPLIT)),
        ],
        compiler_params=pltpu.CompilerParams(vmem_limit_bytes=60 * 1024 * 1024),
        name="last",
    )(cur, left_basis, last)


def solution(mesh):
    return jax.shard_map(
        per_device,
        mesh=mesh,
        in_specs=(
            P(("leaf", "rows"), None),
            P(("leaf", "rows"), None),
            P(("leaf", "rows"), None, None),
            P(None, ("leaf", "rows"), None),
            P(None, ("leaf", "rows"), None),
            P(),
            P(),
        ),
        out_specs=P(("leaf", "rows"), None),
        check_vma=False,
    )
```

```python
import jax
import jax.numpy as jnp
from jax import lax
from jax.experimental import pallas as pl
from jax.experimental.pallas import tpu as pltpu
from jax.sharding import PartitionSpec as P

F32 = jnp.float32
BF16 = jnp.bfloat16
MESH = pl.DeviceIdType.MESH
TN = (((0,), (0,)), ((), ()))
NT = (((1,), (1,)), ((), ()))
NN = (((1,), (0,)), ((), ()))
CHUNKS = 6
PER = 3
CHUNK = 256 * PER
LAST_SPLIT = 4


def mm(a, b, dims=NN):
    return lax.dot_general(a, b, dims, preferred_element_type=F32)


def halves(x):
    hi = x.astype(BF16)
    return hi, (x - hi.astype(F32)).astype(BF16)


def side_by_side(x):
    return jnp.concatenate(halves(x), axis=1)


def mm3(x, w_hi, w_lo):
    hi, lo = halves(x)
    return mm(hi, w_hi) + mm(lo, w_hi) + mm(hi, w_lo)


def one_hot(row, count):
    width = row.shape[1]
    spot = lax.broadcasted_iota(jnp.int32, (count, width), 0)
    return jnp.where(spot == jnp.broadcast_to(row, (count, width)), 1.0, 0.0).astype(BF16)


def rdma(src, dst, ssem, rsem, where):
    return pltpu.make_async_remote_copy(
        src_ref=src, dst_ref=dst, send_sem=ssem, recv_sem=rsem, device_id=where, device_id_type=MESH
    )


def main_kernel(
    rhs_hbm, order_ref, inv_hbm, right_hbm, left_hbm, perm_ref, joined_hbm, cur_hbm, last_ref,
    rhs, inv, right, left, cur, folded, turned, nodes, half_nodes, w_hi, w_lo, pairs, gram, upper,
    coef, share0, shares, rest, mine0, gparts, gsum, ones, pair2, quad3,
    rhs_sem, inv_sem, right_sem, rest_sem, left_sem, node_sem, out_sem,
    s0, r0, sg, rg, sga, rga, sgp, rgp, ss, rs, sc, rc, se, re,
):
    leaf = lax.axis_index("leaf")
    row = lax.axis_index("rows")
    near = {"rows": lax.rem(row + 1, 16)}

    def rows_of(chunk):
        return pl.ds(pl.multiple_of(chunk * CHUNK, CHUNK), CHUNK)

    def load(chunk):
        spot = rows_of(chunk)
        blocks = pl.ds(chunk * PER, PER)
        return (
            pltpu.make_async_copy(rhs_hbm.at[spot], rhs.at[spot], rhs_sem.at[chunk]),
            pltpu.make_async_copy(inv_hbm.at[blocks], inv.at[blocks], inv_sem.at[chunk]),
            pltpu.make_async_copy(
                right_hbm.at[pl.ds(0, 2), spot], right.at[pl.ds(0, 2), spot], right_sem.at[chunk]
            ),
        )

    for chunk in range(2):
        for copy in load(chunk):
            copy.start()
    left_copy = pltpu.make_async_copy(left_hbm.at[pl.ds(0, 3)], left, left_sem)
    rest_copy = pltpu.make_async_copy(right_hbm.at[pl.ds(2, 2)], right.at[pl.ds(2, 2)], rest_sem)
    node_copies = [
        pltpu.make_async_copy(joined_hbm.at[leaf], nodes.at[0], node_sem.at[0]),
        pltpu.make_async_copy(joined_hbm.at[8 + leaf // 2], nodes.at[1], node_sem.at[1]),
    ]
    for level in range(2, 4):
        node = 16 - 16 // 2**level + leaf // 2**level
        side = leaf // 2 ** (level - 1) % 2
        node_copies.append(
            pltpu.make_async_copy(
                joined_hbm.at[node, pl.ds(side * 128, 128)], half_nodes.at[level - 2], node_sem.at[level]
            )
        )

    core = leaf % 2
    chip = leaf - core

    def each_row(body):
        for off in range(1, 16):
            body(lax.rem(row + off, 16))

    def each_owner(body):
        for off in range(1, 16):
            body(core, lax.rem(row + off, 16))
        for off in range(16):
            body(1 - core, lax.rem(row + off, 16))

    def place_of(side, q):
        return {"leaf": chip + side, "rows": q}

    barrier = pltpu.get_barrier_semaphore()
    each_owner(
        lambda side, q: pl.semaphore_signal(barrier, inc=1, device_id=place_of(side, q), device_id_type=MESH)
    )
    for off in range(1, 4):
        pl.semaphore_signal(
            barrier, inc=1, device_id={"leaf": lax.rem(leaf + 2 * off, 8)}, device_id_type=MESH
        )

    def solve_leaves(chunk):
        for i in range(PER):
            block = chunk * PER + i
            spot = slice(block * 256, block * 256 + 256)
            moved = mm(one_hot(order_ref[block : block + 1, :], 256), inv[block], NT).astype(BF16)
            inv[block] = moved
            basis = jnp.concatenate([right[0, spot, :], right[1, spot, :]], axis=1)
            hi, lo = halves(mm(moved, basis))
            part = slice(i * 256, i * 256 + 256)
            folded[chunk % 2, 0, part, :] = hi
            folded[chunk % 2, 1, part, :] = lo
        turned[chunk] = jnp.transpose(rhs[chunk * CHUNK : chunk * CHUNK + CHUNK, :])

    def project_first(chunk):
        cols = turned[chunk]
        terms = mm(jnp.concatenate([cols, cols], axis=1), folded[chunk % 2].reshape(2 * CHUNK, 256))
        pairs[0] = terms if chunk == 0 else pairs[0] + terms

    for chunk in range(CHUNKS):
        for copy in load(chunk):
            copy.wait()
        if chunk + 2 < CHUNKS:
            for copy in load(chunk + 2):
                copy.start()
        else:
            for copy in ((left_copy,), (*node_copies, rest_copy))[chunk + 2 - CHUNKS]:
                copy.start()
        if chunk > 0:
            project_first(chunk - 1)
        solve_leaves(chunk)
    project_first(CHUNKS - 1)

    pl.semaphore_wait(barrier, 34)

    def send0(q):
        src = pairs.at[0, pl.ds(q * 32, 32), pl.ds(0, 128)]
        return rdma(src, share0.at[row], s0, r0, {"rows": q})

    each_row(lambda q: send0(q).start())
    share0[row] = pairs[0, pl.ds(row * 32, 32), 0:128]
    all0 = share0.at[pl.ds(0, 15)]

    left_copy.wait()
    rest_copy.wait()
    gram[...] = jnp.zeros_like(gram)
    pairs[1] = jnp.zeros_like(pairs[1])

    def multiply(step, carry):
        spot = pl.ds(pl.multiple_of(step * 2 * CHUNK, 2 * CHUNK), 2 * CHUNK)

        def both(ref, one, two):
            return jnp.concatenate([ref[one, spot, :], ref[two, spot, :]], axis=1)

        gram[0] += mm(both(left, 0, 1), both(right, 2, 3), TN)
        gram[1] += mm(both(left, 0, 2), both(right, 1, 3), TN)
        return carry

    lax.fori_loop(0, CHUNKS // 2, multiply, 0)
    upper[:, 0:256] = gram[0, 128:256, :]
    upper[:, 256:384] = gram[1, 128:256, 128:256]

    def send_gram(q):
        return rdma(upper.at[pl.ds(q * 8, 8)], gparts.at[row], sg, rg, {"rows": q})

    each_row(lambda q: send_gram(q).start())
    gparts[row] = upper[pl.ds(row * 8, 8), :]

    for copy in node_copies:
        copy.wait()
    start = 0
    for level in range(4):
        hot = one_hot(perm_ref[level : level + 1, :], 128)
        hi, lo = halves(nodes[level] if level < 2 else half_nodes[level - 2])
        count = hi.shape[0]
        for side in range(2):
            cut = slice(side * 128, side * 128 + 128)
            w_hi[cut, start : start + count] = mm(hot, hi[:, cut], NT).astype(BF16)
            w_lo[cut, start : start + count] = mm(hot, lo[:, cut], NT).astype(BF16)
        start += count

    rdma(all0, all0, s0, r0, near).wait_recv()
    low_child = share0[0]
    high_child = share0[8]
    for i in range(1, 8):
        low_child = low_child + share0[i]
        high_child = high_child + share0[8 + i]
    c0 = mm3(jnp.concatenate([low_child, high_child], axis=1), w_hi[:, 0:256], w_lo[:, 0:256])
    mine0[0] = c0[:, 0:128]
    mine0[1] = c0[:, 128:256]
    own = pl.ds(row * 32, 32)

    def send_c0(q):
        return rdma(mine0.at[q // 8], coef.at[0, own], sc.at[0], rc.at[0], {"rows": q})

    each_row(lambda q: send_c0(q).start())
    coef[0, own] = mine0[row // 8]

    def gathered(level):
        spot = coef.at[level, pl.ds(0, 480)]
        rdma(spot, spot, sc.at[level], rc.at[level], near).wait_recv()

    all_parts = gparts.at[pl.ds(0, 15)]
    rdma(all_parts, all_parts, sg, rg, near).wait_recv()
    total = gparts[0]
    for i in range(1, 16):
        total = total + gparts[i]
    own8 = pl.ds(core * 128 + row * 8, 8)
    gsum[own8, :] = total

    def send_sum(q):
        return rdma(gsum.at[own8], gsum.at[own8], sga, rga, {"rows": q})

    each_row(lambda q: send_sum(q).start())

    def project_rest(start, count):
        total = pairs[1]
        for j in range(count):
            chunk = start + j
            parts = []
            for i in range(PER):
                spot = pl.ds(pl.multiple_of(chunk * CHUNK + i * 256, 256), 256)
                basis = jnp.concatenate([right[2, spot, :], right[3, spot, :]], axis=1)
                parts.append(halves(mm(inv[chunk * PER + i], basis)))
            cols = turned[chunk]
            hi = jnp.concatenate([part[0] for part in parts], axis=0)
            lo = jnp.concatenate([part[1] for part in parts], axis=0)
            total = total + mm(jnp.concatenate([cols, cols], axis=1), jnp.concatenate([hi, lo], axis=0))
        pairs[1] = total

    @pl.loop(0, CHUNKS // 2)
    def _(step):
        project_rest(step * 2, 2)

    gathered(0)
    c0_hi, c0_lo = halves(coef[0])

    def send_rest(level, side, q):
        return rdma(
            rest.at[level - 1, pl.ds(q * 32 + side * 16, 16)], shares.at[level - 1, leaf % 2 * 16 + row],
            ss.at[level - 1], rs.at[level - 1], place_of(side, q),
        )

    own16 = pl.ds(row * 32 + core * 16, 16)
    def update(level):
        lanes = slice(128, 256) if level == 3 else slice(0, 128)
        g_hi, g_lo = halves(gram[1 if level == 1 else 0, 0:128, lanes])
        half = slice(level % 2 * 128, level % 2 * 128 + 128)
        taken = mm(c0_hi, g_hi) + mm(c0_lo, g_hi) + mm(c0_hi, g_lo)
        rest[level - 1] = pairs[level // 2, :, half] - taken
        each_owner(lambda side, q: send_rest(level, side, q).start())
        shares[level - 1, core * 16 + row] = rest[level - 1, own16]

    update(1)
    update(2)
    update(3)

    sums = gsum.at[pl.ds(0, 120)]
    rdma(sums, sums, sga, rga, near).wait_recv()
    plane = gsum.at[pl.ds(core * 128, 128)]

    def send_plane():
        return rdma(plane, plane, sgp, rgp, {"leaf": chip + 1 - core})

    send_plane().start()

    first = jnp.concatenate([c0_hi, c0_lo], axis=1)

    def correct_first(chunk, carry):
        for i in range(PER):
            spot = pl.ds(pl.multiple_of(chunk * CHUNK + i * 256, 256), 256)
            basis = left[0, spot, :]
            taken = mm(jnp.concatenate([basis, basis], axis=1), first, NT)
            cur[spot, :] = mm(inv[chunk * PER + i], rhs[spot, :], TN) - taken
        return carry

    lax.fori_loop(0, 4, correct_first, 0)

    def arrived(level):
        spot = shares.at[level - 1, pl.ds(0, 31)]
        rdma(spot, spot, ss.at[level - 1], rs.at[level - 1], near).wait_recv()

    def summed(level, start, count):
        value = shares[level - 1, start]
        for i in range(start + 1, start + count):
            value = value + shares[level - 1, i]
        return value

    def send_c(level, side, q):
        source = ones.at[side] if level == 1 else coef.at[level, own16]
        return rdma(source, coef.at[level, own16], sc.at[level], rc.at[level], place_of(side, q))

    def z_sends(level, buf):
        count = 2 ** (level - 1)
        base = leaf // (2 * count) * (2 * count) + core
        spot = leaf // 2 % count
        return [
            rdma(
                buf.at[spot], buf.at[spot], se.at[level - 2], re.at[level - 2],
                {"leaf": base + 2 * lax.rem(spot + off, count)},
            )
            for off in range(1, count)
        ]

    def begin(level, buf, value):
        buf[leaf // 2 % 2 ** (level - 1)] = value
        for copy in z_sends(level, buf):
            copy.start()

    def finish(level, buf):
        count = 2 ** (level - 1)
        spot = buf.at[pl.ds(0, count - 1)]
        rdma(spot, spot, se.at[level - 2], re.at[level - 2], near).wait_recv()
        half = count // 2
        low, high = buf[0], buf[half]
        for i in range(1, half):
            low = low + buf[i]
            high = high + buf[half + i]
        cut = slice(256 + level * 128, 384 + level * 128)
        c = mm3(jnp.concatenate([low, high], axis=1), w_hi[:, cut], w_lo[:, cut])
        coef[level, own16] = c
        return c

    send_plane().wait_recv()
    g1_hi, g1_lo = halves(gsum[:, 0:256])
    g2_hi, g2_lo = halves(gsum[:, 256:384])
    arrived(1)
    c1 = mm3(
        jnp.concatenate([summed(1, 0, 16), summed(1, 16, 16)], axis=1), w_hi[:, 256:512], w_lo[:, 256:512]
    )
    taken = mm3(c1, g1_hi, g1_lo)
    arrived(2)
    begin(2, pair2, summed(2, 0, 32) - taken[:, 0:128])
    ones[0] = c1[:, 0:128]
    ones[1] = c1[:, 128:256]
    each_owner(lambda side, q: send_c(1, side, q).start())
    coef[1, own16] = ones[core]

    @pl.when(row < 16)
    def _():
        correct_first(4, 0)

    arrived(3)
    part3 = summed(3, 0, 32) - taken[:, 128:256]
    c2 = finish(2, pair2)
    begin(3, quad3, part3 - mm3(jnp.concatenate([c2, c2], axis=1), g2_hi, g2_lo))
    each_owner(lambda side, q: send_c(2, side, q).start())

    @pl.when(row < 16)
    def _():
        correct_first(5, 0)

    finish(3, quad3)
    each_owner(lambda side, q: send_c(3, side, q).start())

    def spread(level):
        spot = coef.at[level, pl.ds(0, 496)]
        return rdma(spot, spot, sc.at[level], rc.at[level], near)

    spread(1).wait_recv()
    spread(2).wait_recv()
    middle = jnp.concatenate([side_by_side(coef[1]), side_by_side(coef[2])], axis=1)

    def store(chunk):
        spot = rows_of(chunk)
        return pltpu.make_async_copy(cur.at[spot], cur_hbm.at[spot], out_sem.at[chunk])

    def correct_middle(chunk, carry):
        spot = rows_of(chunk)
        one, two = left[1, spot, :], left[2, spot, :]
        cur[spot, :] = cur[spot, :] - mm(jnp.concatenate([one, one, two, two], axis=1), middle, NT)
        store(chunk).start()
        return carry

    lax.fori_loop(0, CHUNKS, correct_middle, 0)
    spread(3).wait_recv()
    last_ref[...] = side_by_side(coef[3])

    rdma(all0, all0, s0, r0, near).wait_send()
    rdma(all_parts, all_parts, sg, rg, near).wait_send()
    rdma(sums, sums, sga, rga, near).wait_send()
    send_plane().wait_send()
    span = coef.at[0, pl.ds(0, 480)]
    rdma(span, span, sc.at[0], rc.at[0], near).wait_send()
    for level in range(1, 4):
        spread(level).wait_send()
        span = shares.at[level - 1, pl.ds(0, 31)]
        rdma(span, span, ss.at[level - 1], rs.at[level - 1], near).wait_send()
    for level, buf in ((2, pair2), (3, quad3)):
        span = buf.at[pl.ds(0, 2 ** (level - 1) - 1)]
        rdma(span, span, se.at[level - 2], re.at[level - 2], near).wait_send()
    for chunk in range(CHUNKS):
        store(chunk).wait()


def last_kernel(cur_hbm, left_hbm, last_hbm, out_hbm, cur, left, last, cur_sem, left_sem, last_sem, out_sem):
    part = CHUNK // LAST_SPLIT

    def parts(chunk):
        return [pl.ds(chunk * CHUNK + j * part, part) for j in range(LAST_SPLIT)]

    def reads(chunk):
        rows = pl.ds(chunk * CHUNK, CHUNK)
        copies = [pltpu.make_async_copy(left_hbm.at[3, rows], left.at[rows], left_sem.at[chunk])]
        for j, spot in enumerate(parts(chunk)):
            copies.append(pltpu.make_async_copy(cur_hbm.at[spot], cur.at[spot], cur_sem.at[chunk, j]))
        return copies

    def writes(chunk):
        return [
            pltpu.make_async_copy(cur.at[spot], out_hbm.at[spot], out_sem.at[chunk, j])
            for j, spot in enumerate(parts(chunk))
        ]

    last_copy = pltpu.make_async_copy(last_hbm, last, last_sem)
    last_copy.start()
    for chunk in range(CHUNKS):
        for copy in reads(chunk):
            copy.start()
    last_copy.wait()
    weights = last[...]
    for chunk in range(CHUNKS):
        for copy in reads(chunk):
            copy.wait()
        rows = slice(chunk * CHUNK, chunk * CHUNK + CHUNK)
        basis = left[rows, :]
        cur[rows, :] = cur[rows, :] - mm(jnp.concatenate([basis, basis], axis=1), weights, NT)
        for copy in writes(chunk):
            copy.start()
    for chunk in range(CHUNKS):
        for copy in writes(chunk):
            copy.wait()


def per_device(rhs, leaf_order, leaf_inv, right_basis, left_basis, rank_perm, joined):
    blocks = leaf_inv.shape[0]
    count = rhs.shape[0]
    dma = pltpu.SemaphoreType.DMA
    vmem = pl.BlockSpec(memory_space=pltpu.VMEM)
    hbm = pl.BlockSpec(memory_space=pl.ANY)
    cur, last = pl.pallas_call(
        main_kernel,
        out_shape=(jax.ShapeDtypeStruct(rhs.shape, F32), jax.ShapeDtypeStruct((512, 256), BF16)),
        in_specs=[hbm, vmem, hbm, hbm, hbm, vmem, hbm],
        out_specs=(hbm, vmem),
        scratch_shapes=[
            pltpu.VMEM((count, 512), BF16),
            pltpu.VMEM((blocks, 256, 256), BF16),
            pltpu.VMEM((4, count, 128), BF16),
            pltpu.VMEM((3, count, 128), BF16),
            pltpu.VMEM((count, 512), F32),
            pltpu.VMEM((2, 2, CHUNK, 256), BF16),
            pltpu.VMEM((CHUNKS, 512, CHUNK), BF16),
            pltpu.VMEM((2, 256, 256), F32),
            pltpu.VMEM((2, 128, 256), F32),
            pltpu.VMEM((256, 768), BF16),
            pltpu.VMEM((256, 768), BF16),
            pltpu.VMEM((2, 512, 256), F32),
            pltpu.VMEM((2, 256, 256), F32),
            pltpu.VMEM((128, 384), F32),
            pltpu.VMEM((4, 512, 128), F32),
            pltpu.VMEM((16, 32, 128), F32),
            pltpu.VMEM((3, 32, 16, 128), F32),
            pltpu.VMEM((3, 512, 128), F32),
            pltpu.VMEM((2, 32, 128), F32),
            pltpu.VMEM((16, 8, 384), F32),
            pltpu.VMEM((256, 384), F32),
            pltpu.VMEM((2, 16, 128), F32),
            pltpu.VMEM((2, 16, 128), F32),
            pltpu.VMEM((4, 16, 128), F32),
            dma((CHUNKS,)), dma((CHUNKS,)), dma((CHUNKS,)), dma, dma, dma((4,)), dma((CHUNKS,)),
            dma, dma, dma, dma, dma, dma, dma, dma, dma((3,)), dma((3,)), dma((4,)), dma((4,)), dma((2,)), dma((2,)),
        ],
        compiler_params=pltpu.CompilerParams(
            collective_id=0, has_side_effects=True, vmem_limit_bytes=56 * 1024 * 1024
        ),
        name="main",
    )(rhs, leaf_order, leaf_inv, right_basis, left_basis, rank_perm, joined)

    return pl.pallas_call(
        last_kernel,
        out_shape=jax.ShapeDtypeStruct(rhs.shape, F32),
        in_specs=[hbm, hbm, hbm],
        out_specs=hbm,
        scratch_shapes=[
            pltpu.VMEM((count, 512), F32),
            pltpu.VMEM((count, 128), BF16),
            pltpu.VMEM((512, 256), BF16),
            dma((CHUNKS, LAST_SPLIT)), dma((CHUNKS,)), dma, dma((CHUNKS, LAST_SPLIT)),
        ],
        compiler_params=pltpu.CompilerParams(vmem_limit_bytes=60 * 1024 * 1024),
        name="last",
    )(cur, left_basis, last)


def solution(mesh):
    return jax.shard_map(
        per_device,
        mesh=mesh,
        in_specs=(
            P(("leaf", "rows"), None),
            P(("leaf", "rows"), None),
            P(("leaf", "rows"), None, None),
            P(None, ("leaf", "rows"), None),
            P(None, ("leaf", "rows"), None),
            P(),
            P(),
        ),
        out_specs=P(("leaf", "rows"), None),
        check_vma=False,
    )
```
